512 devices in a mesh: row: 8 (over x, core), col: 64 (over z, y).
Axes of the slice: x: 4, y: 8, z: 8, core: 2. Of those that a mesh axis runs over, the one named last changes fastest.
Arguments:
- src_latent: bfloat16 [32, 32768], P(None, 'row'), may hold values from -6 to 6
- tgt_latent: bfloat16 [32, 131072], P(None, 'col'), may hold values from -6 to 6
- g_start: float32 [131072], P('col'), may hold values from -1.5 to 1.5
- pairs: int32 [8, 64, 8, 2], P('row', 'col'), may hold values from 0 to 7, as said below
- counts: int32 [8, 64], P('row', 'col'), may hold values from 1 to 8, as said below
Outputs:
- f_new: float32 [32768], P('row')
- g_new: float32 [131072], P('col')
- bary: float32 [32, 32768], P(None, 'row')
The draws below stay inside these ranges and needn't reach their ends.
Inputs may be any that keep to these rules, and one draw needn't show every extreme that they name: Within one device's 8 slots all pairs are distinct; entry 0 is below 8 and entry 1 below 4. Every source block and every target block appears among the live slots of some device. `counts`: some device has exactly 8 live slots in every draw.
All inputs are finite; a program needn't handle non-finite values.
Results may differ from the reference program's by a relative error of at most 0.0012.
Values sent between devices are 32-bit elements; how exact they have to be, the bound alone decides.
No kernel may reach another device: no remote copies, remote signals or barrier semaphores. Data moves between devices by JAX's collectives and lax.ppermute only.
A program may use at most 64 MiB of HBM per device.

```python
import jax
import jax.numpy as jnp
from jax import lax

DIM = 32
BLOCK = 512
SB = 8
TB = 4
PAIRS = 8
NS = 32768
NT = 131072
N_ROW = 8
N_COL = 64


def draw_counts(key, part):
    key = jax.random.fold_in(key, 11)
    devices_all = N_ROW * N_COL
    raw = jax.random.randint(key, (devices_all,), 0, PAIRS)
    cover = (SB + N_COL - 1) // N_COL
    loads = jnp.maximum(1 + raw * raw // PAIRS, cover)
    busiest = jax.random.randint(jax.random.fold_in(key, 7), (), 0, devices_all)
    loads = jnp.where(jnp.arange(devices_all) == busiest, PAIRS, loads)
    return loads.reshape(N_ROW, N_COL).astype(jnp.int32)


def draw_pairs(key, part):
    key = jax.random.fold_in(key, 13)
    cells = SB * TB
    cover = (SB + N_COL - 1) // N_COL
    rr = jnp.arange(N_ROW, dtype=jnp.int32)[:, None, None]
    cc = jnp.arange(N_COL, dtype=jnp.int32)[None, :, None]
    kk = jnp.arange(cover, dtype=jnp.int32)[None, None, :]
    forced_id = (cc + N_COL * kk) % SB * TB + (rr + kk) % TB
    ids = jnp.arange(cells, dtype=jnp.int32)
    forced = jnp.any(ids[None, None, None, :] == forced_id[..., None], axis=2)
    scores = jax.random.randint(key, (N_ROW, N_COL, cells), 0, 2 ** 20) * cells + ids[None, None, :]
    sort_key = jnp.where(forced, ids[None, None, :], cells + scores)
    order = jnp.argsort(sort_key, axis=-1)[..., :PAIRS].astype(jnp.int32)
    return jnp.stack([order // TB, order % TB], axis=-1).astype(jnp.int32)


def shard_levels(rng, dims, cuts, least, top_value):
    def one(position, shards_of):
        steps = jax.random.uniform(jax.random.fold_in(jax.random.fold_in(rng, 6), position), (shards_of,), jnp.float32, least / len(cuts), top_value / len(cuts))
        return jnp.repeat(jnp.exp(steps), dims[position] // shards_of).reshape((-1,) + (1,) * (len(dims) - position - 1))

    loudness = one(*cuts[0])
    for cut in cuts[1:]:
        loudness = loudness * one(*cut)
    return loudness


def scatter_about(own_key, dims, spread, bound, cuts=(), kind=jnp.bfloat16):
    factor_of = shard_levels(own_key, dims, cuts, -0.22, 0.18) if cuts else 1.0
    result = jax.random.normal(own_key, dims, jnp.float32) * spread * factor_of
    return jnp.minimum(jnp.maximum(result, -bound), bound).astype(kind)


def setup_inputs(seed: int = 0) -> dict:
    key_of = jax.random.split(jax.random.key(seed), 6)
    return {
        "src_latent": scatter_about(key_of[0], (DIM, NS), 1.0, 6.0, ((1, 8),)),
        "tgt_latent": scatter_about(key_of[1], (DIM, NT), 1.0, 6.0, ((1, 64),)),
        "g_start": scatter_about(key_of[2], (NT,), 0.25, 1.5, ((0, 64),), jnp.float32),
        "pairs": draw_pairs(jax.random.fold_in(key_of[5], 71), 0),
        "counts": draw_counts(jax.random.fold_in(key_of[5], 71), 0),
    }


epsilon = 0.01
very_low = -1e30


def tile_score(src_latent, tgt_latent, sq_src, sq_tgt, s_off, t_off, row_pot, col_pot):
    xs = lax.dynamic_slice_in_dim(src_latent, s_off, BLOCK, 1)
    ys = lax.dynamic_slice_in_dim(tgt_latent, t_off, BLOCK, 1)
    cross = lax.dot_general(xs, ys, (((0,), (0,)), ((), ())), preferred_element_type=jnp.float32)
    sx = lax.dynamic_slice_in_dim(sq_src, s_off, BLOCK)
    sy = lax.dynamic_slice_in_dim(sq_tgt, t_off, BLOCK)
    cost = (sx[:, None] + sy[None, :] - 2.0 * cross) / DIM
    shifted = -cost
    if row_pot is not None:
        shifted = shifted + lax.dynamic_slice_in_dim(row_pot, s_off, BLOCK)[:, None]
    if col_pot is not None:
        shifted = shifted + lax.dynamic_slice_in_dim(col_pot, t_off, BLOCK)[None, :]
    return shifted / epsilon, ys


def reference(src_latent, tgt_latent, g_start, pairs, counts):
    sq_src = jnp.sum(jnp.square(src_latent.astype(jnp.float32)), axis=0)
    sq_tgt = jnp.sum(jnp.square(tgt_latent.astype(jnp.float32)), axis=0)
    rr = jnp.arange(N_ROW, dtype=jnp.int32)[:, None, None]
    cc = jnp.arange(N_COL, dtype=jnp.int32)[None, :, None]
    pp = jnp.arange(PAIRS, dtype=jnp.int32)[None, None, :]
    s_offs = ((rr * SB + pairs[..., 0]) * BLOCK).reshape(-1).astype(jnp.int32)
    t_offs = ((cc * TB + pairs[..., 1]) * BLOCK).reshape(-1).astype(jnp.int32)
    live = (pp < counts[:, :, None]).reshape(-1)
    items = (s_offs, t_offs, live)

    def score_of(s_off, t_off, row_pot, col_pot):
        return tile_score(src_latent, tgt_latent, sq_src, sq_tgt, s_off, t_off, row_pot, col_pot)

    def peaks(row_pot, col_pot, axis, length):
        def step(peak, item):
            s_off, t_off, valid = item
            score, _ = score_of(s_off, t_off, row_pot, col_pot)
            off = s_off if axis == 1 else t_off
            red = jnp.where(valid, jnp.max(score, axis=axis), very_low)
            old = lax.dynamic_slice_in_dim(peak, off, BLOCK)
            return lax.dynamic_update_slice_in_dim(peak, jnp.maximum(old, red), off, 0), None
        return lax.scan(step, jnp.full((length,), very_low, jnp.float32), items)[0]

    def totals(row_pot, col_pot, axis, length, peak):
        def step(total, item):
            s_off, t_off, valid = item
            score, _ = score_of(s_off, t_off, row_pot, col_pot)
            off = s_off if axis == 1 else t_off
            pk = lax.dynamic_slice_in_dim(peak, off, BLOCK)
            pk = pk[:, None] if axis == 1 else pk[None, :]
            red = jnp.where(valid, jnp.sum(jnp.exp(score - pk), axis=axis), 0.0)
            old = lax.dynamic_slice_in_dim(total, off, BLOCK)
            return lax.dynamic_update_slice_in_dim(total, old + red, off, 0), None
        return lax.scan(step, jnp.zeros((length,), jnp.float32), items)[0]

    peak_f = peaks(None, g_start, 1, NS)
    total_f = totals(None, g_start, 1, NS, peak_f)
    f_new = -epsilon * jnp.log(1.0 * NS) - epsilon * (peak_f + jnp.log(total_f))
    peak_g = peaks(f_new, None, 0, NT)
    total_g = totals(f_new, None, 0, NT, peak_g)
    g_new = -epsilon * jnp.log(1.0 * NT) - epsilon * (peak_g + jnp.log(total_g))
    peak_b = peaks(None, g_new, 1, NS)

    def step(carry, item):
        numer, denom = carry
        s_off, t_off, valid = item
        score, ys = score_of(s_off, t_off, None, g_new)
        pk = lax.dynamic_slice_in_dim(peak_b, s_off, BLOCK)
        weight = jnp.where(valid, jnp.exp(score - pk[:, None]), 0.0).astype(jnp.bfloat16)
        part = lax.dot_general(ys, weight, (((1,), (1,)), ((), ())), preferred_element_type=jnp.float32)
        old = lax.dynamic_slice_in_dim(numer, s_off, BLOCK, 1)
        numer = lax.dynamic_update_slice_in_dim(numer, old + part, s_off, 1)
        oldd = lax.dynamic_slice_in_dim(denom, s_off, BLOCK)
        denom = lax.dynamic_update_slice_in_dim(denom, oldd + jnp.sum(weight.astype(jnp.float32), axis=1), s_off, 0)
        return (numer, denom), None

    init = (jnp.zeros((DIM, NS), jnp.float32), jnp.zeros((NS,), jnp.float32))
    numer, denom = lax.scan(step, init, items)[0]
    bary = numer / denom[None, :]
    return f_new, g_new, bary
```

```python
import functools
import math

import jax
import jax.numpy as jnp
from jax import lax
from jax.experimental import pallas as pl
from jax.experimental.pallas import tpu as pltpu
from jax.sharding import PartitionSpec as P

BLOCK = 512
LANES = 128
DIM = 32
DEPTH = 80

epsilon = 0.01
very_low = -1e30
cross_scale = 2.0 / (DIM * epsilon)
square_scale = 1.0 / (DIM * epsilon)

F32 = jnp.float32
BF16 = jnp.bfloat16


def pieces(vec):
    first = vec.astype(BF16).astype(F32)
    rest = vec - first
    second = rest.astype(BF16).astype(F32)
    return first, second, rest - second


def bias_rows(vec):
    row = lax.broadcasted_iota(jnp.int32, (16, vec.shape[1]), 0)
    a, b, c = pieces(vec)
    return jnp.where(row == 0, a, jnp.where(row == 1, b, jnp.where(row == 2, c, 0.0))).astype(BF16)


def one_rows(width):
    row = lax.broadcasted_iota(jnp.int32, (16, width), 0)
    return jnp.where(row < 3, 1.0, 0.0).astype(BF16)


def fill_src(x_ref, xa):
    for b in range(xa.shape[0]):
        xs = x_ref[:, b * BLOCK : (b + 1) * BLOCK].astype(F32) * cross_scale
        high = xs.astype(BF16)
        xa[b, 0:32, :] = high
        xa[b, 32:64, :] = (xs - high.astype(F32)).astype(BF16)


def fill_tgt(y_ref, ya):
    for b in range(ya.shape[0]):
        ys = y_ref[:, b * BLOCK : (b + 1) * BLOCK]
        ya[b, 0:32, :] = ys
        ya[b, 32:64, :] = ys


def tile_scores(left, right):
    return lax.dot_general(left, right, (((0,), (0,)), ((), ())), preferred_element_type=F32)


def online(score, top_ref, total_ref, at):
    old = top_ref[at]
    top = jnp.maximum(old, jnp.max(score, axis=0, keepdims=True))
    weight = jnp.exp(score - top)
    keep = jnp.exp(old - top)
    total_ref[at] = total_ref[at] * keep + jnp.sum(weight, axis=0, keepdims=True)
    top_ref[at] = top


def clear(top_ref, total_ref):
    top_ref[...] = jnp.full(top_ref.shape, very_low, F32)
    total_ref[...] = jnp.zeros(total_ref.shape, F32)


def spread_rows(top_ref, total_ref, out_ref, copies):
    per = BLOCK // LANES
    rows = top_ref.shape[0] * per
    for b in range(top_ref.shape[0]):
        total = total_ref[b]
        lse = jnp.where(total > 0.0, top_ref[b] + jnp.log(total), very_low)
        for k in range(per):
            out_ref[b * per + k : b * per + k + 1, :] = lse[:, k * LANES : (k + 1) * LANES]
    value = out_ref[0:rows, :]
    for c in range(1, copies):
        out_ref[c * rows : (c + 1) * rows, :] = value


def merged(in_ref, parts):
    rows = in_ref.shape[0] // parts
    values = [in_ref[c * rows : (c + 1) * rows, :] for c in range(parts)]
    top = functools.reduce(jnp.maximum, values)
    total = functools.reduce(jnp.add, [jnp.exp(v - top) for v in values])
    return top + jnp.log(total)


def src_kernel(parts, slots, count, x_ref, y_ref, g_ref, out_ref, xa, ya, top_ref, total_ref):
    fill_src(x_ref, xa)
    fill_tgt(y_ref, ya)
    for b in range(xa.shape[0]):
        xa[b, 64:80, :] = one_rows(BLOCK)
    for b in range(ya.shape[0]):
        ys = y_ref[:, b * BLOCK : (b + 1) * BLOCK].astype(F32)
        square = jnp.sum(ys * ys, axis=0, keepdims=True)
        start = g_ref[:, b * BLOCK : (b + 1) * BLOCK]
        ya[b, 64:80, :] = bias_rows(start / epsilon - square * square_scale)
    clear(top_ref, total_ref)

    def step(p, carry):
        s, t = slots[2 * p], slots[2 * p + 1]
        online(tile_scores(ya[t], xa[s]), top_ref, total_ref, s)
        return carry

    lax.fori_loop(0, count[0], step, 0)
    spread_rows(top_ref, total_ref, out_ref, parts)


def merge_kernel(parts, in_ref, out_ref):
    value = merged(in_ref, parts)
    rows = value.shape[0]
    for c in range(parts):
        out_ref[c * rows : (c + 1) * rows, :] = value


def tgt_kernel(parts, copies, log_rows, slots, count, in_ref, x_ref, y_ref, f_ref, out_ref, xa, ya, top_ref, total_ref):
    fill_src(x_ref, xa)
    fill_tgt(y_ref, ya)
    for b in range(ya.shape[0]):
        ya[b, 64:80, :] = one_rows(BLOCK)
    bias = -log_rows - merged(in_ref, parts)
    per = BLOCK // LANES
    for b in range(xa.shape[0]):
        xs = x_ref[:, b * BLOCK : (b + 1) * BLOCK].astype(F32)
        square = jnp.sum(xs * xs, axis=0, keepdims=True)
        for k in range(per):
            row = b * per + k
            lanes = slice(k * LANES, (k + 1) * LANES)
            one = bias[row : row + 1, :]
            xa[b, 64:80, lanes] = bias_rows(one)
            f_ref[row : row + 1, :] = epsilon * one + square[:, lanes] * (1.0 / DIM)
    clear(top_ref, total_ref)

    def step(p, carry):
        s, t = slots[2 * p], slots[2 * p + 1]
        online(tile_scores(xa[s], ya[t]), top_ref, total_ref, t)
        return carry

    lax.fori_loop(0, count[0], step, 0)
    spread_rows(top_ref, total_ref, out_ref, copies)


def bary_kernel(parts, log_cols, slots, count, in_ref, x_ref, y_ref, g_ref, out_ref, xa, ya, yb, top_ref, acc_ref):
    fill_src(x_ref, xa)
    fill_tgt(y_ref, ya)
    for b in range(xa.shape[0]):
        xa[b, 64:80, :] = one_rows(BLOCK)
    bias = -log_cols - merged(in_ref, parts)
    per = BLOCK // LANES
    first_row = lax.broadcasted_iota(jnp.int32, (16, BLOCK), 0) == 0
    for b in range(ya.shape[0]):
        y_block = y_ref[:, b * BLOCK : (b + 1) * BLOCK]
        ys = y_block.astype(F32)
        square = jnp.sum(ys * ys, axis=0, keepdims=True)
        yb[b, 0:32, :] = y_block
        yb[b, 32:48, :] = jnp.where(first_row, 1.0, 0.0).astype(BF16)
        for k in range(per):
            row = b * per + k
            lanes = slice(k * LANES, (k + 1) * LANES)
            one = bias[row : row + 1, :]
            ya[b, 64:80, lanes] = bias_rows(one)
            g_ref[row : row + 1, :] = epsilon * one + square[:, lanes] * (1.0 / DIM)
    top_ref[...] = jnp.full(top_ref.shape, very_low, F32)
    acc_ref[...] = jnp.zeros(acc_ref.shape, F32)

    def step(p, carry):
        s, t = slots[2 * p], slots[2 * p + 1]
        score = tile_scores(ya[t], xa[s])
        old = top_ref[s]
        top = jnp.maximum(old, jnp.max(score, axis=0, keepdims=True))
        weight = jnp.exp(score - top).astype(BF16)
        part = jnp.dot(yb[t], weight, preferred_element_type=F32)
        acc_ref[s] = acc_ref[s] * jnp.exp(old - top) + part
        top_ref[s] = top
        return carry

    lax.fori_loop(0, count[0], step, 0)
    for b in range(top_ref.shape[0]):
        total = acc_ref[b, 32:33, :]
        live = total > 0.0
        lse = jnp.where(live, top_ref[b] + jnp.log(total), very_low)
        mean = acc_ref[b, 0:32, :] * jnp.where(live, 1.0 / total, 0.0)
        for k in range(per):
            lanes = slice(k * LANES, (k + 1) * LANES)
            for h in range(2):
                at = ((b * per + k) * 2 + h) * 17
                out_ref[at : at + 16, :] = mean[h * 16 : h * 16 + 16, lanes]
                out_ref[at + 16 : at + 17, :] = lse[:, lanes]


def mean_kernel(parts, in_ref, out_ref):
    logs = [in_ref[c * 17 + 16 : c * 17 + 17, :] for c in range(parts)]
    top = functools.reduce(jnp.maximum, logs)
    total = jnp.zeros_like(top)
    value = jnp.zeros((16, LANES), F32)
    for c in range(parts):
        weight = jnp.exp(logs[c] - top)
        total = total + weight
        value = value + weight * in_ref[c * 17 : c * 17 + 16, :]
    value = value / total
    for c in range(parts):
        out_ref[c * 16 : (c + 1) * 16, :] = value


def place_kernel(in_ref, out_ref):
    for c in range(in_ref.shape[0] // 16):
        k, h = c // 2, c % 2
        out_ref[h * 16 : (h + 1) * 16, k * LANES : (k + 1) * LANES] = in_ref[c * 16 : (c + 1) * 16, :]


def whole(count):
    return [pl.BlockSpec(memory_space=pltpu.VMEM)] * count


def scalars():
    return [pl.BlockSpec(memory_space=pltpu.SMEM)] * 2


def body(src_latent, tgt_latent, g_start, pairs, counts):
    src_len = src_latent.shape[1]
    tgt_len = tgt_latent.shape[1]
    n_row, n_col = lax.axis_size("row"), lax.axis_size("col")
    side = 8
    other = n_col // side
    groups_z = [[z * side + y for z in range(other)] for y in range(side)]
    groups_y = [[z * side + y for y in range(side)] for z in range(other)]
    slots = pairs.reshape(-1)
    count = counts.reshape(-1)
    s_blocks, t_blocks = src_len // BLOCK, tgt_len // BLOCK
    s_rows, t_rows = src_len // LANES, tgt_len // LANES
    log_rows = math.log(src_len * n_row)
    log_cols = math.log(tgt_len * n_col)

    def aug(blocks):
        return pltpu.VMEM((blocks, DEPTH, BLOCK), BF16)

    def line(blocks):
        return pltpu.VMEM((blocks, 1, BLOCK), F32)

    def exchange(x, axis, parts, groups=None):
        width = x.shape[0] // parts * LANES
        y = lax.all_to_all(
            x.reshape(parts, width), axis, 0, 0, axis_index_groups=groups, tiled=True
        )
        return y.reshape(-1, LANES)

    def rows_of(n):
        return jax.ShapeDtypeStruct((n, LANES), F32)

    lse = pl.pallas_call(
        functools.partial(src_kernel, other),
        out_shape=rows_of(other * s_rows),
        in_specs=scalars() + whole(3),
        out_specs=whole(1)[0],
        scratch_shapes=[aug(s_blocks), aug(t_blocks), line(s_blocks), line(s_blocks)],
        name="src_pass",
    )(slots, count, src_latent, tgt_latent, g_start.reshape(1, -1))
    lse = exchange(lse, "col", other, groups_z)
    lse = pl.pallas_call(
        functools.partial(merge_kernel, other),
        out_shape=rows_of(side * s_rows),
        in_specs=whole(1),
        out_specs=whole(1)[0],
        name="src_merge",
    )(lse)
    lse = exchange(lse, "col", side, groups_y)
    f_new, lse = pl.pallas_call(
        functools.partial(tgt_kernel, side, n_row, log_rows),
        out_shape=(rows_of(s_rows), rows_of(n_row * t_rows)),
        in_specs=scalars() + whole(3),
        out_specs=tuple(whole(2)),
        scratch_shapes=[aug(s_blocks), aug(t_blocks), line(t_blocks), line(t_blocks)],
        name="tgt_pass",
    )(slots, count, lse, src_latent, tgt_latent)
    lse = exchange(lse, "row", n_row)
    g_new, means = pl.pallas_call(
        functools.partial(bary_kernel, n_row, log_cols),
        out_shape=(rows_of(t_rows), rows_of(n_col * 17)),
        in_specs=scalars() + whole(3),
        out_specs=tuple(whole(2)),
        scratch_shapes=[
            aug(s_blocks),
            aug(t_blocks),
            pltpu.VMEM((t_blocks, 48, BLOCK), BF16),
            line(s_blocks),
            pltpu.VMEM((s_blocks, 48, BLOCK), F32),
        ],
        name="bary_pass",
    )(slots, count, lse, src_latent, tgt_latent)
    means = exchange(means, "col", n_col)
    means = pl.pallas_call(
        functools.partial(mean_kernel, n_col),
        out_shape=rows_of(n_col * 16),
        in_specs=whole(1),
        out_specs=whole(1)[0],
        name="bary_merge",
    )(means)
    means = exchange(means, "col", n_col)
    bary = pl.pallas_call(
        place_kernel,
        out_shape=jax.ShapeDtypeStruct((DIM, src_len), F32),
        in_specs=whole(1),
        out_specs=whole(1)[0],
        name="bary_place",
    )(means)
    return f_new.reshape(-1), g_new.reshape(-1), bary


def solution(mesh):
    in_specs = (
        P(None, "row"),
        P(None, "col"),
        P("col"),
        P("row", "col", None, None),
        P("row", "col"),
    )
    out_specs = (P("row"), P("col"), P(None, "row"))
    return jax.shard_map(body, mesh=mesh, in_specs=in_specs, out_specs=out_specs, check_vma=False)
```

```python
import functools
import math

import jax
import jax.numpy as jnp
from jax import lax
from jax.experimental import pallas as pl
from jax.experimental.pallas import tpu as pltpu
from jax.sharding import PartitionSpec as P

BLOCK = 512
LANES = 128
DIM = 32
DEPTH = 80
PACK = 18
VMEM_LIMIT = 16 * 2**20

epsilon = 0.01
very_low = -1e30
cross_scale = 2.0 / (DIM * epsilon)
square_scale = 1.0 / (DIM * epsilon)

F32 = jnp.float32
BF16 = jnp.bfloat16


def pieces(vec):
    first = vec.astype(BF16).astype(F32)
    rest = vec - first
    second = rest.astype(BF16).astype(F32)
    return first, second, rest - second


def bias_rows(vec):
    row = lax.broadcasted_iota(jnp.int32, (16, vec.shape[1]), 0)
    a, b, c = pieces(vec)
    return jnp.where(row == 0, a, jnp.where(row == 1, b, jnp.where(row == 2, c, 0.0))).astype(BF16)


def one_rows(width):
    row = lax.broadcasted_iota(jnp.int32, (16, width), 0)
    return jnp.where(row < 3, 1.0, 0.0).astype(BF16)


def fill_src(x_ref, xa):
    for b in range(xa.shape[0]):
        xs = x_ref[:, b * BLOCK : (b + 1) * BLOCK].astype(F32) * cross_scale
        high = xs.astype(BF16)
        xa[b, 0:32, :] = high
        xa[b, 32:64, :] = (xs - high.astype(F32)).astype(BF16)


def fill_tgt(y_ref, ya):
    for b in range(ya.shape[0]):
        ys = y_ref[:, b * BLOCK : (b + 1) * BLOCK]
        ya[b, 0:32, :] = ys
        ya[b, 32:64, :] = ys


def tile_scores(left, right):
    return lax.dot_general(left, right, (((0,), (0,)), ((), ())), preferred_element_type=F32)


def online(score, top_ref, total_ref, at):
    old = top_ref[at]
    top = jnp.maximum(old, jnp.max(score, axis=0, keepdims=True))
    weight = jnp.exp(score - top)
    keep = jnp.exp(old - top)
    total_ref[at] = total_ref[at] * keep + jnp.sum(weight, axis=0, keepdims=True)
    top_ref[at] = top


def clear(top_ref, total_ref):
    top_ref[...] = jnp.full(top_ref.shape, very_low, F32)
    total_ref[...] = jnp.zeros(total_ref.shape, F32)


def spread_rows(top_ref, total_ref, out_ref, copies):
    per = BLOCK // LANES
    rows = top_ref.shape[0] * per
    for b in range(top_ref.shape[0]):
        total = total_ref[b]
        lse = jnp.where(total > 0.0, top_ref[b] + jnp.log(total), very_low)
        for k in range(per):
            out_ref[b * per + k : b * per + k + 1, :] = lse[:, k * LANES : (k + 1) * LANES]
    value = out_ref[0:rows, :]
    for c in range(1, copies):
        out_ref[c * rows : (c + 1) * rows, :] = value


def merged(in_ref, parts):
    rows = in_ref.shape[0] // parts
    values = [in_ref[c * rows : (c + 1) * rows, :] for c in range(parts)]
    top = functools.reduce(jnp.maximum, values)
    total = functools.reduce(jnp.add, [jnp.exp(v - top) for v in values])
    return top + jnp.log(total)


def src_kernel(parts, slots, count, x_ref, y_ref, g_ref, out_ref, xa, ya, top_ref, total_ref):
    fill_src(x_ref, xa)
    fill_tgt(y_ref, ya)
    for b in range(xa.shape[0]):
        xa[b, 64:80, :] = one_rows(BLOCK)
    for b in range(ya.shape[0]):
        ys = y_ref[:, b * BLOCK : (b + 1) * BLOCK].astype(F32)
        square = jnp.sum(ys * ys, axis=0, keepdims=True)
        start = g_ref[:, b * BLOCK : (b + 1) * BLOCK]
        ya[b, 64:80, :] = bias_rows(start / epsilon - square * square_scale)
    clear(top_ref, total_ref)

    def step(p, carry):
        s, t = slots[0, p], slots[1, p]
        online(tile_scores(ya[t], xa[s]), top_ref, total_ref, s)
        return carry

    lax.fori_loop(0, count[0, 0], step, 0)
    spread_rows(top_ref, total_ref, out_ref, parts)


def merge_kernel(parts, in_ref, out_ref):
    value = merged(in_ref, parts)
    rows = value.shape[0]
    for c in range(parts):
        out_ref[c * rows : (c + 1) * rows, :] = value


def tgt_kernel(parts, copies, log_rows, slots, count, in_ref, x_ref, y_ref, f_ref, out_ref, xa, ya, top_ref, total_ref):
    fill_src(x_ref, xa)
    fill_tgt(y_ref, ya)
    for b in range(ya.shape[0]):
        ya[b, 64:80, :] = one_rows(BLOCK)
    bias = -log_rows - merged(in_ref, parts)
    per = BLOCK // LANES
    for b in range(xa.shape[0]):
        xs = x_ref[:, b * BLOCK : (b + 1) * BLOCK].astype(F32)
        square = jnp.sum(xs * xs, axis=0, keepdims=True)
        for k in range(per):
            row = b * per + k
            lanes = slice(k * LANES, (k + 1) * LANES)
            one = bias[row : row + 1, :]
            xa[b, 64:80, lanes] = bias_rows(one)
            f_ref[row : row + 1, :] = epsilon * one + square[:, lanes] * (1.0 / DIM)
    clear(top_ref, total_ref)

    def step(p, carry):
        s, t = slots[0, p], slots[1, p]
        online(tile_scores(xa[s], ya[t]), top_ref, total_ref, t)
        return carry

    lax.fori_loop(0, count[0, 0], step, 0)
    spread_rows(top_ref, total_ref, out_ref, copies)


def bary_kernel(parts, log_cols, slots, count, in_ref, x_ref, y_ref, g_ref, out_ref, xa, ya, yb, top_ref, acc_ref):
    fill_src(x_ref, xa)
    fill_tgt(y_ref, ya)
    for b in range(xa.shape[0]):
        xa[b, 64:80, :] = one_rows(BLOCK)
    bias = -log_cols - merged(in_ref, parts)
    per = BLOCK // LANES
    first_row = lax.broadcasted_iota(jnp.int32, (16, BLOCK), 0) == 0
    for b in range(ya.shape[0]):
        y_block = y_ref[:, b * BLOCK : (b + 1) * BLOCK]
        ys = y_block.astype(F32)
        square = jnp.sum(ys * ys, axis=0, keepdims=True)
        yb[b, 0:32, :] = y_block
        yb[b, 32:48, :] = jnp.where(first_row, 1.0, 0.0).astype(BF16)
        for k in range(per):
            row = b * per + k
            lanes = slice(k * LANES, (k + 1) * LANES)
            one = bias[row : row + 1, :]
            ya[b, 64:80, lanes] = bias_rows(one)
            g_ref[row : row + 1, :] = epsilon * one + square[:, lanes] * (1.0 / DIM)
    top_ref[...] = jnp.full(top_ref.shape, very_low, F32)
    acc_ref[...] = jnp.zeros(acc_ref.shape, F32)

    def step(p, carry):
        s, t = slots[0, p], slots[1, p]
        score = tile_scores(ya[t], xa[s])
        old = top_ref[s]
        top = jnp.maximum(old, jnp.max(score, axis=0, keepdims=True))
        weight = jnp.exp(score - top).astype(BF16)
        part = jnp.dot(yb[t], weight, preferred_element_type=F32)
        acc_ref[s] = acc_ref[s] * jnp.exp(old - top) + part
        top_ref[s] = top
        return carry

    lax.fori_loop(0, count[0, 0], step, 0)
    for b in range(top_ref.shape[0]):
        total = acc_ref[b, 32:33, :]
        live = total > 0.0
        lse = jnp.where(live, top_ref[b] + jnp.log(total), very_low)
        mean = acc_ref[b, 0:32, :] * jnp.where(live, 1.0 / total, 0.0)
        for h in range(DIM // 8):
            for k in range(per):
                lanes = slice(k * LANES, (k + 1) * LANES)
                owner = (h * top_ref.shape[0] * per + b * per + k) // 2
                at = owner * PACK + k % 2 * 8
                out_ref[at : at + 8, :] = mean[h * 8 : h * 8 + 8, lanes]
                at = owner * PACK + 16 + k % 2
                out_ref[at : at + 1, :] = lse[:, lanes]


def mean_kernel(parts, in_ref, out_ref):
    for half in range(2):
        logs = [in_ref[c * PACK + 16 + half : c * PACK + 17 + half, :] for c in range(parts)]
        top = functools.reduce(jnp.maximum, logs)
        total = jnp.zeros_like(top)
        value = jnp.zeros((8, LANES), F32)
        for c in range(parts):
            weight = jnp.exp(logs[c] - top)
            total = total + weight
            at = c * PACK + half * 8
            value = value + weight * in_ref[at : at + 8, :]
        value = value / total
        for c in range(parts):
            at = c * 16 + half * 8
            out_ref[at : at + 8, :] = value


def whole(count):
    return [pl.BlockSpec(memory_space=pltpu.VMEM)] * count


def scalars():
    return [pl.BlockSpec(memory_space=pltpu.SMEM)] * 2


def body(src_latent, tgt_latent, g_start, pairs, counts):
    src_len = src_latent.shape[1]
    tgt_len = tgt_latent.shape[1]
    n_row, n_col = lax.axis_size("row"), lax.axis_size("col")
    side = 8
    other = n_col // side
    groups_z = [[z * side + y for z in range(other)] for y in range(side)]
    groups_y = [[z * side + y for y in range(side)] for z in range(other)]
    slots = pairs.reshape(pairs.shape[2:]).T
    count = counts
    s_blocks, t_blocks = src_len // BLOCK, tgt_len // BLOCK
    s_rows, t_rows = src_len // LANES, tgt_len // LANES
    log_rows = math.log(src_len * n_row)
    log_cols = math.log(tgt_len * n_col)

    def aug(blocks):
        return pltpu.VMEM((blocks, DEPTH, BLOCK), BF16)

    def line(blocks):
        return pltpu.VMEM((blocks, 1, BLOCK), F32)

    def exchange(x, axis, parts, groups=None):
        width = x.shape[0] // parts * LANES
        y = lax.all_to_all(
            x.reshape(parts, width), axis, 0, 0, axis_index_groups=groups, tiled=True
        )
        return y.reshape(-1, LANES)

    def rows_of(n):
        return jax.ShapeDtypeStruct((n, LANES), F32)

    lse = pl.pallas_call(
        functools.partial(src_kernel, other),
        out_shape=rows_of(other * s_rows),
        in_specs=scalars() + whole(3),
        out_specs=whole(1)[0],
        scratch_shapes=[aug(s_blocks), aug(t_blocks), line(s_blocks), line(s_blocks)],
        compiler_params=pltpu.CompilerParams(vmem_limit_bytes=VMEM_LIMIT),
        name="src_pass",
    )(slots, count, src_latent, tgt_latent, g_start.reshape(1, -1))
    lse = exchange(lse, "col", other, groups_z)
    lse = pl.pallas_call(
        functools.partial(merge_kernel, other),
        out_shape=rows_of(side * s_rows),
        in_specs=whole(1),
        out_specs=whole(1)[0],
        compiler_params=pltpu.CompilerParams(vmem_limit_bytes=VMEM_LIMIT),
        name="src_merge",
    )(lse)
    lse = exchange(lse, "col", side, groups_y)
    f_new, lse = pl.pallas_call(
        functools.partial(tgt_kernel, side, n_row, log_rows),
        out_shape=(rows_of(s_rows), rows_of(n_row * t_rows)),
        in_specs=scalars() + whole(3),
        out_specs=tuple(whole(2)),
        scratch_shapes=[aug(s_blocks), aug(t_blocks), line(t_blocks), line(t_blocks)],
        compiler_params=pltpu.CompilerParams(vmem_limit_bytes=VMEM_LIMIT),
        name="tgt_pass",
    )(slots, count, lse, src_latent, tgt_latent)
    lse = exchange(lse, "row", n_row)
    g_new, means = pl.pallas_call(
        functools.partial(bary_kernel, n_row, log_cols),
        out_shape=(rows_of(t_rows), rows_of(n_col * PACK)),
        in_specs=scalars() + whole(3),
        out_specs=tuple(whole(2)),
        scratch_shapes=[
            aug(s_blocks),
            aug(t_blocks),
            pltpu.VMEM((t_blocks, 48, BLOCK), BF16),
            line(s_blocks),
            pltpu.VMEM((s_blocks, 48, BLOCK), F32),
        ],
        compiler_params=pltpu.CompilerParams(vmem_limit_bytes=VMEM_LIMIT),
        name="bary_pass",
    )(slots, count, lse, src_latent, tgt_latent)
    means = exchange(means, "col", n_col)
    means = pl.pallas_call(
        functools.partial(mean_kernel, n_col),
        out_shape=rows_of(n_col * 16),
        in_specs=whole(1),
        out_specs=whole(1)[0],
        compiler_params=pltpu.CompilerParams(vmem_limit_bytes=VMEM_LIMIT),
        name="bary_merge",
    )(means)
    means = exchange(means, "col", n_col)
    tiles = means.reshape(DIM // 8, s_rows, 8, LANES)
    bary = tiles.transpose(0, 2, 1, 3).reshape(DIM, src_len)
    return f_new.reshape(-1), g_new.reshape(-1), bary


def solution(mesh):
    in_specs = (
        P(None, "row"),
        P(None, "col"),
        P("col"),
        P("row", "col", None, None),
        P("row", "col"),
    )
    out_specs = (P("row"), P("col"), P(None, "row"))
    return jax.shard_map(body, mesh=mesh, in_specs=in_specs, out_specs=out_specs, check_vma=False)
```

```python
import functools
import math

import jax
import jax.numpy as jnp
from jax import lax
from jax.experimental import pallas as pl
from jax.experimental.pallas import tpu as pltpu
from jax.sharding import PartitionSpec as P

BLOCK = 512
LANES = 128
DIM = 32
DEPTH = 112
PACK = 18
VMEM_LIMIT = 16 * 2**20

epsilon = 0.01
very_low = -1e30
log2e = math.log2(math.e)
unit = epsilon / log2e
cross_scale = 2.0 / (DIM * unit)
square_scale = 1.0 / (DIM * unit)

F32 = jnp.float32
BF16 = jnp.bfloat16


def pieces(vec):
    first = vec.astype(BF16).astype(F32)
    rest = vec - first
    second = rest.astype(BF16).astype(F32)
    return first, second, rest - second


def bias_rows(vec):
    row = lax.broadcasted_iota(jnp.int32, (16, vec.shape[1]), 0)
    a, b, c = pieces(vec)
    return jnp.where(row == 0, a, jnp.where(row == 1, b, jnp.where(row == 2, c, 0.0))).astype(BF16)


def one_rows(width):
    row = lax.broadcasted_iota(jnp.int32, (16, width), 0)
    return jnp.where(row < 3, 1.0, 0.0).astype(BF16)


def fill_src(x_ref, xa):
    for b in range(xa.shape[0]):
        xs = x_ref[:, b * BLOCK : (b + 1) * BLOCK].astype(F32) * cross_scale
        for k, piece in enumerate(pieces(xs)):
            xa[b, k * DIM : (k + 1) * DIM, :] = piece.astype(BF16)


def fill_tgt(y_ref, ya):
    for b in range(ya.shape[0]):
        ys = y_ref[:, b * BLOCK : (b + 1) * BLOCK]
        for k in range(3):
            ya[b, k * DIM : (k + 1) * DIM, :] = ys


def tile_scores(left, right):
    return lax.dot_general(left, right, (((0,), (0,)), ((), ())), preferred_element_type=F32)


CHUNK = 128


UNROLL = 2


def tile_lse(left, right):
    top = total = None
    scores = tile_scores(left, right)
    for c in range(0, BLOCK, CHUNK):
        score = scores[c : c + CHUNK, :].reshape(CHUNK // 8, 8, BLOCK)
        most = jnp.max(score, axis=0)
        old, top = top, most if c == 0 else jnp.maximum(top, most)
        part = jnp.sum(jnp.exp2(score - top), axis=0)
        total = part if c == 0 else total * jnp.exp2(old - top) + part
    return top, total


def add_tile(tile, top_ref, total_ref, at):
    top, total = tile
    old = top_ref[at]
    most = jnp.maximum(old, top)
    total_ref[at] = total_ref[at] * jnp.exp2(old - most) + total * jnp.exp2(top - most)
    top_ref[at] = most


def lse_tiles(count, slots, left_of, right_of, at_of, spare, top_ref, total_ref):
    def step(q, carry):
        tiles = []
        for u in range(UNROLL):
            p = q * UNROLL + u
            live = p < count
            p = jnp.minimum(p, count - 1)
            s, t = slots[0, p], slots[1, p]
            tiles.append((tile_lse(left_of(s, t), right_of(s, t)), jnp.where(live, at_of(s, t), spare)))
        for tile, at in tiles:
            add_tile(tile, top_ref, total_ref, at)
        return carry

    lax.fori_loop(0, lax.div(count + UNROLL - 1, UNROLL), step, 0)


def joined(top, total):
    most = jnp.max(top, axis=0, keepdims=True)
    total = jnp.sum(total * jnp.exp2(top - most), axis=0, keepdims=True)
    return jnp.where(total > 0.0, most + jnp.log2(total), very_low)


def clear(top_ref, total_ref):
    top_ref[...] = jnp.full(top_ref.shape, very_low, F32)
    total_ref[...] = jnp.zeros(total_ref.shape, F32)


def spread_rows(blocks, top_ref, total_ref, out_ref, copies):
    per = BLOCK // LANES
    rows = blocks * per
    for b in range(blocks):
        lse = joined(top_ref[b], total_ref[b])
        for k in range(per):
            out_ref[b * per + k : b * per + k + 1, :] = lse[:, k * LANES : (k + 1) * LANES]
    value = out_ref[0:rows, :]
    for c in range(1, copies):
        out_ref[c * rows : (c + 1) * rows, :] = value


def merged(in_ref, parts):
    rows = in_ref.shape[0] // parts
    values = [in_ref[c * rows : (c + 1) * rows, :] for c in range(parts)]
    top = functools.reduce(jnp.maximum, values)
    total = functools.reduce(jnp.add, [jnp.exp2(v - top) for v in values])
    return top + jnp.log2(total)


def fetch(sources, targets, sems):
    copies = [
        pltpu.make_async_copy(source, target, sems.at[k])
        for k, (source, target) in enumerate(zip(sources, targets))
    ]
    for copy in copies:
        copy.start()
    return copies


def src_kernel(parts, count, slots_in, x_in, y_in, g_in, out_ref, slots, x_ref, y_ref, g_ref, sems, xa, ya, top_ref, total_ref):
    copies = fetch(
        (x_in, y_in, g_in, slots_in), (x_ref, y_ref, g_ref, slots), sems
    )
    for b in range(xa.shape[0]):
        xa[b, 3 * DIM : DEPTH, :] = one_rows(BLOCK)
    clear(top_ref, total_ref)
    for copy in copies:
        copy.wait()
    fill_src(x_ref, xa)
    fill_tgt(y_ref, ya)
    for b in range(ya.shape[0]):
        ys = y_ref[:, b * BLOCK : (b + 1) * BLOCK].astype(F32)
        square = jnp.sum(ys * ys, axis=0, keepdims=True)
        start = g_ref[:, b * BLOCK : (b + 1) * BLOCK]
        ya[b, 3 * DIM : DEPTH, :] = bias_rows(start / unit - square * square_scale)

    lse_tiles(
        count[0, 0],
        slots,
        lambda s, t: ya[t],
        lambda s, t: xa[s],
        lambda s, t: s,
        xa.shape[0],
        top_ref,
        total_ref,
    )
    spread_rows(xa.shape[0], top_ref, total_ref, out_ref, parts)


def merge_kernel(parts, in_ref, out_ref):
    value = merged(in_ref, parts)
    rows = value.shape[0]
    for c in range(parts):
        out_ref[c * rows : (c + 1) * rows, :] = value


def tgt_kernel(parts, copies, log_rows, slots, count, in_ref, x_ref, y_ref, f_ref, out_ref, xa, ya, top_ref, total_ref):
    fill_src(x_ref, xa)
    fill_tgt(y_ref, ya)
    for b in range(ya.shape[0]):
        ya[b, 3 * DIM : DEPTH, :] = one_rows(BLOCK)
    bias = -log_rows - merged(in_ref, parts)
    per = BLOCK // LANES
    for b in range(xa.shape[0]):
        xs = x_ref[:, b * BLOCK : (b + 1) * BLOCK].astype(F32)
        square = jnp.sum(xs * xs, axis=0, keepdims=True)
        for k in range(per):
            row = b * per + k
            lanes = slice(k * LANES, (k + 1) * LANES)
            one = bias[row : row + 1, :]
            xa[b, 3 * DIM : DEPTH, lanes] = bias_rows(one)
            f_ref[row : row + 1, :] = unit * one + square[:, lanes] * (1.0 / DIM)
    clear(top_ref, total_ref)

    lse_tiles(
        count[0, 0],
        slots,
        lambda s, t: xa[s],
        lambda s, t: ya[t],
        lambda s, t: t,
        ya.shape[0],
        top_ref,
        total_ref,
    )
    spread_rows(ya.shape[0], top_ref, total_ref, out_ref, copies)


def bary_kernel(parts, log_cols, slots, count, in_ref, x_ref, y_ref, g_ref, out_ref, xa, ya, yb, top_ref, acc_ref):
    fill_src(x_ref, xa)
    fill_tgt(y_ref, ya)
    for b in range(xa.shape[0]):
        xa[b, 3 * DIM : DEPTH, :] = one_rows(BLOCK)
    bias = -log_cols - merged(in_ref, parts)
    per = BLOCK // LANES
    first_row = lax.broadcasted_iota(jnp.int32, (16, BLOCK), 0) == 0
    for b in range(ya.shape[0]):
        y_block = y_ref[:, b * BLOCK : (b + 1) * BLOCK]
        ys = y_block.astype(F32)
        square = jnp.sum(ys * ys, axis=0, keepdims=True)
        yb[b, 0:32, :] = y_block
        yb[b, 32:48, :] = jnp.where(first_row, 1.0, 0.0).astype(BF16)
        for k in range(per):
            row = b * per + k
            lanes = slice(k * LANES, (k + 1) * LANES)
            one = bias[row : row + 1, :]
            ya[b, 3 * DIM : DEPTH, lanes] = bias_rows(one)
            g_ref[row : row + 1, :] = unit * one + square[:, lanes] * (1.0 / DIM)
    top_ref[...] = jnp.full(top_ref.shape, very_low, F32)
    acc_ref[...] = jnp.zeros(acc_ref.shape, F32)

    spare = xa.shape[0]

    def step(q, carry):
        tiles = []
        for u in range(2):
            p = q * 2 + u
            live = p < count[0, 0]
            p = jnp.minimum(p, count[0, 0] - 1)
            s, t = slots[0, p], slots[1, p]
            scores = tile_scores(ya[t], xa[s])
            top = part = None
            for c in range(0, BLOCK, 128):
                score = scores[c : c + 128, :]
                most = jnp.max(score, axis=0, keepdims=True)
                old, top = top, most if c == 0 else jnp.maximum(top, most)
                weight = jnp.exp2(score - top).astype(BF16)
                more = jnp.dot(yb[t, :, c : c + 128], weight, preferred_element_type=F32)
                part = more if c == 0 else part * jnp.exp2(old - top) + more
            tiles.append((top, part, jnp.where(live, s, spare)))
        for top, part, at in tiles:
            old = top_ref[at]
            most = jnp.maximum(old, top)
            acc_ref[at] = acc_ref[at] * jnp.exp2(old - most) + part * jnp.exp2(top - most)
            top_ref[at] = most
        return carry

    lax.fori_loop(0, lax.div(count[0, 0] + 2 - 1, 2), step, 0)
    for b in range(spare):
        total = acc_ref[b, 32:33, :]
        live = total > 0.0
        lse = jnp.where(live, top_ref[b] + jnp.log2(total), very_low)
        mean = acc_ref[b, 0:32, :] * jnp.where(live, 1.0 / total, 0.0)
        for h in range(DIM // 8):
            for k in range(per):
                lanes = slice(k * LANES, (k + 1) * LANES)
                owner = (h * spare * per + b * per + k) // 2
                at = owner * PACK + k % 2 * 8
                out_ref[at : at + 8, :] = mean[h * 8 : h * 8 + 8, lanes]
                at = owner * PACK + 16 + k % 2
                out_ref[at : at + 1, :] = lse[:, lanes]


def mean_kernel(parts, in_ref, out_ref):
    for half in range(2):
        logs = [in_ref[c * PACK + 16 + half : c * PACK + 17 + half, :] for c in range(parts)]
        top = functools.reduce(jnp.maximum, logs)
        total = jnp.zeros_like(top)
        value = jnp.zeros((8, LANES), F32)
        for c in range(parts):
            weight = jnp.exp2(logs[c] - top)
            total = total + weight
            at = c * PACK + half * 8
            value = value + weight * in_ref[at : at + 8, :]
        value = value / total
        for c in range(parts):
            at = c * 16 + half * 8
            out_ref[at : at + 8, :] = value


def whole(count):
    return [pl.BlockSpec(memory_space=pltpu.VMEM)] * count


def scalars():
    return [pl.BlockSpec(memory_space=pltpu.SMEM)] * 2


def body(src_latent, tgt_latent, g_start, pairs, counts):
    src_len = src_latent.shape[1]
    tgt_len = tgt_latent.shape[1]
    n_row, n_col = lax.axis_size("row"), lax.axis_size("col")
    side = 8
    other = n_col // side
    groups_z = [[z * side + y for z in range(other)] for y in range(side)]
    groups_y = [[z * side + y for y in range(side)] for z in range(other)]
    slots = pairs.reshape(pairs.shape[2:]).T
    count = counts
    s_blocks, t_blocks = src_len // BLOCK, tgt_len // BLOCK
    s_rows, t_rows = src_len // LANES, tgt_len // LANES
    log_rows = math.log2(src_len * n_row)
    log_cols = math.log2(tgt_len * n_col)

    def aug(blocks):
        return pltpu.VMEM((blocks, DEPTH, BLOCK), BF16)

    def line(blocks, rows=8):
        return pltpu.VMEM((blocks, rows, BLOCK), F32)

    def exchange(x, axis, parts, groups=None):
        width = x.shape[0] // parts * LANES
        y = lax.all_to_all(
            x.reshape(parts, width), axis, 0, 0, axis_index_groups=groups, tiled=True
        )
        return y.reshape(-1, LANES)

    def rows_of(n):
        return jax.ShapeDtypeStruct((n, LANES), F32)

    lse = pl.pallas_call(
        functools.partial(src_kernel, other),
        out_shape=rows_of(other * s_rows),
        in_specs=scalars()[:1] + [pl.BlockSpec(memory_space=pltpu.HBM)] * 4,
        out_specs=whole(1)[0],
        scratch_shapes=[
            pltpu.SMEM(slots.shape, jnp.int32),
            pltpu.VMEM(src_latent.shape, BF16),
            pltpu.VMEM(tgt_latent.shape, BF16),
            pltpu.VMEM((1, tgt_len), F32),
            pltpu.SemaphoreType.DMA((4,)),
            aug(s_blocks), aug(t_blocks), line(s_blocks + 1), line(s_blocks + 1)],
        compiler_params=pltpu.CompilerParams(vmem_limit_bytes=VMEM_LIMIT),
        name="src_pass",
    )(count, *[
        pltpu.with_memory_space_constraint(a, pltpu.HBM)
        for a in (slots, src_latent, tgt_latent, g_start.reshape(1, -1))
    ])
    lse = exchange(lse, "col", other, groups_z)
    lse = pl.pallas_call(
        functools.partial(merge_kernel, other),
        out_shape=rows_of(side * s_rows),
        in_specs=whole(1),
        out_specs=whole(1)[0],
        compiler_params=pltpu.CompilerParams(vmem_limit_bytes=VMEM_LIMIT),
        name="src_merge",
    )(lse)
    lse = exchange(lse, "col", side, groups_y)
    f_new, lse = pl.pallas_call(
        functools.partial(tgt_kernel, side, n_row, log_rows),
        out_shape=(rows_of(s_rows), rows_of(n_row * t_rows)),
        in_specs=scalars() + whole(3),
        out_specs=tuple(whole(2)),
        scratch_shapes=[aug(s_blocks), aug(t_blocks), line(t_blocks + 1), line(t_blocks + 1)],
        compiler_params=pltpu.CompilerParams(vmem_limit_bytes=VMEM_LIMIT),
        name="tgt_pass",
    )(slots, count, lse, src_latent, tgt_latent)
    lse = exchange(lse, "row", n_row)
    g_new, means = pl.pallas_call(
        functools.partial(bary_kernel, n_row, log_cols),
        out_shape=(rows_of(t_rows), rows_of(n_col * PACK)),
        in_specs=scalars() + whole(3),
        out_specs=tuple(whole(2)),
        scratch_shapes=[
            aug(s_blocks),
            aug(t_blocks),
            pltpu.VMEM((t_blocks, 48, BLOCK), BF16),
            line(s_blocks + 1, 1),
            pltpu.VMEM((s_blocks + 1, 48, BLOCK), F32),
        ],
        compiler_params=pltpu.CompilerParams(vmem_limit_bytes=VMEM_LIMIT),
        name="bary_pass",
    )(slots, count, lse, src_latent, tgt_latent)
    means = exchange(means, "col", n_col)
    means = pl.pallas_call(
        functools.partial(mean_kernel, n_col),
        out_shape=rows_of(n_col * 16),
        in_specs=whole(1),
        out_specs=whole(1)[0],
        compiler_params=pltpu.CompilerParams(vmem_limit_bytes=VMEM_LIMIT),
        name="bary_merge",
    )(means)
    means = exchange(means, "col", n_col)
    tiles = means.reshape(DIM // 8, s_rows, 8, LANES)
    bary = tiles.transpose(0, 2, 1, 3).reshape(DIM, src_len)
    return f_new.reshape(-1), g_new.reshape(-1), bary


def solution(mesh):
    in_specs = (
        P(None, "row"),
        P(None, "col"),
        P("col"),
        P("row", "col", None, None),
        P("row", "col"),
    )
    out_specs = (P("row"), P("col"), P(None, "row"))
    return jax.shard_map(body, mesh=mesh, in_specs=in_specs, out_specs=out_specs, check_vma=False)
```

```python
import functools
import math

import jax
import jax.numpy as jnp
from jax import lax
from jax.experimental import pallas as pl
from jax.experimental.pallas import tpu as pltpu
from jax.sharding import PartitionSpec as P

BLOCK = 512
LANES = 128
DIM = 32
DEPTH = 112
PACK = 17
VMEM_LIMIT = 16 * 2**20

epsilon = 0.01
very_low = -1e30
log2e = math.log2(math.e)
unit = epsilon / log2e
cross_scale = 2.0 / (DIM * unit)
square_scale = 1.0 / (DIM * unit)

F32 = jnp.float32
BF16 = jnp.bfloat16


def pieces(vec):
    first = vec.astype(BF16).astype(F32)
    rest = vec - first
    second = rest.astype(BF16).astype(F32)
    return first, second, rest - second


def bias_rows(vec):
    row = lax.broadcasted_iota(jnp.int32, (16, vec.shape[1]), 0)
    a, b, c = pieces(vec)
    return jnp.where(row == 0, a, jnp.where(row == 1, b, jnp.where(row == 2, c, 0.0))).astype(BF16)


def one_rows(width):
    row = lax.broadcasted_iota(jnp.int32, (16, width), 0)
    return jnp.where(row < 3, 1.0, 0.0).astype(BF16)


def fill_src(x_ref, xa):
    for b in range(xa.shape[0]):
        xs = x_ref[:, b * BLOCK : (b + 1) * BLOCK].astype(F32) * cross_scale
        for k, piece in enumerate(pieces(xs)):
            xa[b, k * DIM : (k + 1) * DIM, :] = piece.astype(BF16)


def fill_tgt(y_ref, ya):
    for b in range(ya.shape[0]):
        ys = y_ref[:, b * BLOCK : (b + 1) * BLOCK]
        for k in range(3):
            ya[b, k * DIM : (k + 1) * DIM, :] = ys


def tile_scores(left, right):
    return lax.dot_general(left, right, (((0,), (0,)), ((), ())), preferred_element_type=F32)


CHUNK = 128


UNROLL = 2


def tile_lse(left, right):
    top = total = None
    scores = tile_scores(left, right)
    for c in range(0, BLOCK, CHUNK):
        score = scores[c : c + CHUNK, :].reshape(CHUNK // 8, 8, BLOCK)
        most = jnp.max(score, axis=0)
        old, top = top, most if c == 0 else jnp.maximum(top, most)
        part = jnp.sum(jnp.exp2(score - top), axis=0)
        total = part if c == 0 else total * jnp.exp2(old - top) + part
    return top, total


def add_tile(tile, top_ref, total_ref, at):
    top, total = tile
    old = top_ref[at]
    most = jnp.maximum(old, top)
    total_ref[at] = total_ref[at] * jnp.exp2(old - most) + total * jnp.exp2(top - most)
    top_ref[at] = most


def lse_tiles(count, slots, left_of, right_of, at_of, spare, top_ref, total_ref):
    def step(q, carry):
        tiles = []
        for u in range(UNROLL):
            p = q * UNROLL + u
            live = p < count
            p = jnp.minimum(p, count - 1)
            s, t = slots[0, p], slots[1, p]
            tiles.append((tile_lse(left_of(s, t), right_of(s, t)), jnp.where(live, at_of(s, t), spare)))
        for tile, at in tiles:
            add_tile(tile, top_ref, total_ref, at)
        return carry

    lax.fori_loop(0, lax.div(count + UNROLL - 1, UNROLL), step, 0)


def joined(top, total):
    most = jnp.max(top, axis=0, keepdims=True)
    total = jnp.sum(total * jnp.exp2(top - most), axis=0, keepdims=True)
    return jnp.where(total > 0.0, most + jnp.log2(total), very_low)


def clear(top_ref, total_ref):
    top_ref[...] = jnp.full(top_ref.shape, very_low, F32)
    total_ref[...] = jnp.zeros(total_ref.shape, F32)


def spread_rows(blocks, top_ref, total_ref, out_ref, copies):
    per = BLOCK // LANES
    rows = blocks * per
    for b in range(blocks):
        lse = joined(top_ref[b], total_ref[b])
        for k in range(per):
            out_ref[b * per + k : b * per + k + 1, :] = lse[:, k * LANES : (k + 1) * LANES]
    value = out_ref[0:rows, :]
    for c in range(1, copies):
        out_ref[c * rows : (c + 1) * rows, :] = value


def merged(in_ref, parts):
    rows = in_ref.shape[0] // parts
    values = [in_ref[c * rows : (c + 1) * rows, :] for c in range(parts)]
    top = functools.reduce(jnp.maximum, values)
    total = functools.reduce(jnp.add, [jnp.exp2(v - top) for v in values])
    return top + jnp.log2(total)


def fetch(sources, targets, sems):
    copies = [
        pltpu.make_async_copy(source, target, sems.at[k])
        for k, (source, target) in enumerate(zip(sources, targets))
    ]
    for copy in copies:
        copy.start()
    return copies


def src_kernel(parts, count, slots_in, x_in, y_in, g_in, out_ref, slots, x_ref, y_ref, g_ref, sems, xa, ya, top_ref, total_ref):
    copies = fetch(
        (x_in, y_in, g_in, slots_in), (x_ref, y_ref, g_ref, slots), sems
    )
    for b in range(xa.shape[0]):
        xa[b, 3 * DIM : DEPTH, :] = one_rows(BLOCK)
    clear(top_ref, total_ref)
    for copy in copies:
        copy.wait()
    fill_src(x_ref, xa)
    fill_tgt(y_ref, ya)
    for b in range(ya.shape[0]):
        ys = y_ref[:, b * BLOCK : (b + 1) * BLOCK].astype(F32)
        square = jnp.sum(ys * ys, axis=0, keepdims=True)
        start = g_ref[:, b * BLOCK : (b + 1) * BLOCK]
        ya[b, 3 * DIM : DEPTH, :] = bias_rows(start / unit - square * square_scale)

    lse_tiles(
        count[0, 0],
        slots,
        lambda s, t: ya[t],
        lambda s, t: xa[s],
        lambda s, t: s,
        xa.shape[0],
        top_ref,
        total_ref,
    )
    spread_rows(xa.shape[0], top_ref, total_ref, out_ref, parts)


def merge_kernel(parts, in_ref, out_ref):
    value = merged(in_ref, parts)
    rows = value.shape[0]
    for c in range(parts):
        out_ref[c * rows : (c + 1) * rows, :] = value


def tgt_kernel(parts, copies, log_rows, count, slots_in, in_ref, x_ref, y_ref, f_out, out_ref, slots, f_ref, sems, xa, ya, top_ref, total_ref):
    fetched = fetch((slots_in,), (slots,), sems)[0]
    fill_src(x_ref, xa)
    fill_tgt(y_ref, ya)
    for b in range(ya.shape[0]):
        ya[b, 3 * DIM : DEPTH, :] = one_rows(BLOCK)
    bias = -log_rows - merged(in_ref, parts)
    per = BLOCK // LANES
    for b in range(xa.shape[0]):
        xs = x_ref[:, b * BLOCK : (b + 1) * BLOCK].astype(F32)
        square = jnp.sum(xs * xs, axis=0, keepdims=True)
        for k in range(per):
            row = b * per + k
            lanes = slice(k * LANES, (k + 1) * LANES)
            one = bias[row : row + 1, :]
            xa[b, 3 * DIM : DEPTH, lanes] = bias_rows(one)
            f_ref[row : row + 1, :] = unit * one + square[:, lanes] * (1.0 / DIM)
    written = pltpu.make_async_copy(f_ref, f_out, sems.at[1])
    clear(top_ref, total_ref)
    fetched.wait()
    written.start()

    lse_tiles(
        count[0, 0],
        slots,
        lambda s, t: xa[s],
        lambda s, t: ya[t],
        lambda s, t: t,
        ya.shape[0],
        top_ref,
        total_ref,
    )
    spread_rows(ya.shape[0], top_ref, total_ref, out_ref, copies)
    written.wait()


def bary_kernel(parts, log_cols, count, slots_in, in_ref, x_ref, y_ref, g_out, out_ref, slots, g_ref, sems, xa, ya, yb, top_ref, acc_ref):
    fetched = fetch((slots_in,), (slots,), sems)[0]
    fill_src(x_ref, xa)
    fill_tgt(y_ref, ya)
    for b in range(xa.shape[0]):
        xa[b, 3 * DIM : DEPTH, :] = one_rows(BLOCK)
    bias = -log_cols - merged(in_ref, parts)
    per = BLOCK // LANES
    first_row = lax.broadcasted_iota(jnp.int32, (16, BLOCK), 0) == 0
    for b in range(ya.shape[0]):
        y_block = y_ref[:, b * BLOCK : (b + 1) * BLOCK]
        ys = y_block.astype(F32)
        square = jnp.sum(ys * ys, axis=0, keepdims=True)
        yb[b, 0:32, :] = y_block
        yb[b, 32:48, :] = jnp.where(first_row, 1.0, 0.0).astype(BF16)
        for k in range(per):
            row = b * per + k
            lanes = slice(k * LANES, (k + 1) * LANES)
            one = bias[row : row + 1, :]
            ya[b, 3 * DIM : DEPTH, lanes] = bias_rows(one)
            g_ref[row : row + 1, :] = unit * one + square[:, lanes] * (1.0 / DIM)
    written = pltpu.make_async_copy(g_ref, g_out, sems.at[1])
    top_ref[...] = jnp.full(top_ref.shape, very_low, F32)
    acc_ref[...] = jnp.zeros(acc_ref.shape, F32)

    fetched.wait()
    written.start()
    spare = xa.shape[0]

    def step(q, carry):
        tiles = []
        for u in range(2):
            p = q * 2 + u
            live = p < count[0, 0]
            p = jnp.minimum(p, count[0, 0] - 1)
            s, t = slots[0, p], slots[1, p]
            scores = tile_scores(ya[t], xa[s])
            top = part = None
            for c in range(0, BLOCK, 128):
                score = scores[c : c + 128, :]
                most = jnp.max(score, axis=0, keepdims=True)
                old, top = top, most if c == 0 else jnp.maximum(top, most)
                weight = jnp.exp2(score - top).astype(BF16)
                more = jnp.dot(yb[t, :, c : c + 128], weight, preferred_element_type=F32)
                part = more if c == 0 else part * jnp.exp2(old - top) + more
            tiles.append((top, part, jnp.where(live, s, spare)))
        for top, part, at in tiles:
            old = top_ref[at]
            most = jnp.maximum(old, top)
            acc_ref[at] = acc_ref[at] * jnp.exp2(old - most) + part * jnp.exp2(top - most)
            top_ref[at] = most
        return carry

    lax.fori_loop(0, lax.div(count[0, 0] + 2 - 1, 2), step, 0)
    for b in range(spare):
        total = acc_ref[b, 32:33, :]
        live = total > 0.0
        lse = jnp.where(live, top_ref[b] + jnp.log2(total), very_low)
        mean = acc_ref[b, 0:32, :] * jnp.where(live, 1.0 / total, 0.0)
        for k in range(per):
            lanes = slice(k * LANES, (k + 1) * LANES)
            for h in range(2):
                at = ((b * per + k) * 2 + h) * PACK
                out_ref[at : at + 16, :] = mean[h * 16 : h * 16 + 16, lanes]
                out_ref[at + 16 : at + 17, :] = lse[:, lanes]
    written.wait()

def mean_kernel(parts, in_ref, out_ref):
    logs = [in_ref[c * PACK + 16 : c * PACK + 17, :] for c in range(parts)]
    top = functools.reduce(jnp.maximum, logs)
    total = jnp.zeros_like(top)
    value = jnp.zeros((16, LANES), F32)
    for c in range(parts):
        weight = jnp.exp2(logs[c] - top)
        total = total + weight
        value = value + weight * in_ref[c * PACK : c * PACK + 16, :]
    value = value / total
    for c in range(parts):
        out_ref[c * 16 : (c + 1) * 16, :] = value


def place_kernel(in_ref, out_ref, sems):
    half = in_ref.shape[0] // 2
    copies = []
    for d in range(4):
        for k in range(2):
            runs = pl.ds(k * half, half)
            copies.append(
                pltpu.make_async_copy(
                    in_ref.at[runs, d // 2, d % 2], out_ref.at[d, runs], sems.at[2 * d + k]
                )
            )
    for copy in copies:
        copy.start()
    for copy in copies:
        copy.wait()


def whole(count):
    return [pl.BlockSpec(memory_space=pltpu.VMEM)] * count


def scalar():
    return pl.BlockSpec(memory_space=pltpu.SMEM)


def far():
    return pl.BlockSpec(memory_space=pltpu.HBM)


def body(src_latent, tgt_latent, g_start, pairs, counts):
    src_len = src_latent.shape[1]
    tgt_len = tgt_latent.shape[1]
    n_row, n_col = lax.axis_size("row"), lax.axis_size("col")
    side = 8
    other = n_col // side
    groups_z = [[z * side + y for z in range(other)] for y in range(side)]
    groups_y = [[z * side + y for y in range(side)] for z in range(other)]
    slots = pltpu.with_memory_space_constraint(pairs.reshape(pairs.shape[2:]).T, pltpu.HBM)
    count = counts
    s_blocks, t_blocks = src_len // BLOCK, tgt_len // BLOCK
    s_rows, t_rows = src_len // LANES, tgt_len // LANES
    log_rows = math.log2(src_len * n_row)
    log_cols = math.log2(tgt_len * n_col)

    def aug(blocks):
        return pltpu.VMEM((blocks, DEPTH, BLOCK), BF16)

    def line(blocks, rows=8):
        return pltpu.VMEM((blocks, rows, BLOCK), F32)

    def side_refs(rows):
        return (
            pltpu.SMEM(slots.shape, jnp.int32),
            pltpu.VMEM((rows, LANES), F32),
            pltpu.SemaphoreType.DMA((2,)),
        )

    def exchange(x, axis, parts, groups=None):
        width = x.shape[0] // parts * LANES
        y = lax.all_to_all(
            x.reshape(parts, width), axis, 0, 0, axis_index_groups=groups, tiled=True
        )
        return y.reshape(-1, LANES)

    def rows_of(n):
        return jax.ShapeDtypeStruct((n, LANES), F32)

    lse = pl.pallas_call(
        functools.partial(src_kernel, other),
        out_shape=rows_of(other * s_rows),
        in_specs=[scalar()] + [far()] * 4,
        out_specs=whole(1)[0],
        scratch_shapes=[
            pltpu.SMEM(slots.shape, jnp.int32),
            pltpu.VMEM(src_latent.shape, BF16),
            pltpu.VMEM(tgt_latent.shape, BF16),
            pltpu.VMEM((1, tgt_len), F32),
            pltpu.SemaphoreType.DMA((4,)),
            aug(s_blocks), aug(t_blocks), line(s_blocks + 1), line(s_blocks + 1)],
        compiler_params=pltpu.CompilerParams(vmem_limit_bytes=VMEM_LIMIT),
        name="src_pass",
    )(count, slots, *[
        pltpu.with_memory_space_constraint(a, pltpu.HBM)
        for a in (src_latent, tgt_latent, g_start.reshape(1, -1))
    ])
    lse = exchange(lse, "col", other, groups_z)
    lse = pl.pallas_call(
        functools.partial(merge_kernel, other),
        out_shape=rows_of(side * s_rows),
        in_specs=whole(1),
        out_specs=whole(1)[0],
        compiler_params=pltpu.CompilerParams(vmem_limit_bytes=VMEM_LIMIT),
        name="src_merge",
    )(lse)
    lse = exchange(lse, "col", side, groups_y)
    f_new, lse = pl.pallas_call(
        functools.partial(tgt_kernel, side, n_row, log_rows),
        out_shape=(rows_of(s_rows), rows_of(n_row * t_rows)),
        in_specs=[scalar(), far()] + whole(3),
        out_specs=(far(), whole(1)[0]),
        scratch_shapes=[*side_refs(s_rows), aug(s_blocks), aug(t_blocks), line(t_blocks + 1), line(t_blocks + 1)],
        compiler_params=pltpu.CompilerParams(vmem_limit_bytes=VMEM_LIMIT),
        name="tgt_pass",
    )(count, slots, lse, src_latent, tgt_latent)
    lse = exchange(lse, "row", n_row)
    g_new, means = pl.pallas_call(
        functools.partial(bary_kernel, n_row, log_cols),
        out_shape=(rows_of(t_rows), rows_of(n_col * PACK)),
        in_specs=[scalar(), far()] + whole(3),
        out_specs=(far(), whole(1)[0]),
        scratch_shapes=[
            *side_refs(t_rows),
            aug(s_blocks),
            aug(t_blocks),
            pltpu.VMEM((t_blocks, 48, BLOCK), BF16),
            line(s_blocks + 1, 1),
            pltpu.VMEM((s_blocks + 1, 48, BLOCK), F32),
        ],
        compiler_params=pltpu.CompilerParams(vmem_limit_bytes=VMEM_LIMIT),
        name="bary_pass",
    )(count, slots, lse, src_latent, tgt_latent)
    means = exchange(means, "col", n_col)
    means = pl.pallas_call(
        functools.partial(mean_kernel, n_col),
        out_shape=rows_of(n_col * 16),
        in_specs=whole(1),
        out_specs=whole(1)[0],
        compiler_params=pltpu.CompilerParams(vmem_limit_bytes=VMEM_LIMIT),
        name="bary_merge",
    )(means)
    means = exchange(means, "col", n_col)
    tiles = pl.pallas_call(
        place_kernel,
        out_shape=jax.ShapeDtypeStruct((DIM // 8, s_rows, 8, LANES), F32),
        in_specs=whole(1),
        out_specs=far(),
        scratch_shapes=[pltpu.SemaphoreType.DMA((8,))],
        compiler_params=pltpu.CompilerParams(vmem_limit_bytes=VMEM_LIMIT),
        name="bary_place",
    )(means.reshape(s_rows, 2, 2, 8, LANES))
    bary = tiles.transpose(0, 2, 1, 3).reshape(DIM, src_len)
    return f_new.reshape(-1), g_new.reshape(-1), bary


def solution(mesh):
    in_specs = (
        P(None, "row"),
        P(None, "col"),
        P("col"),
        P("row", "col", None, None),
        P("row", "col"),
    )
    out_specs = (P("row"), P("col"), P(None, "row"))
    return jax.shard_map(body, mesh=mesh, in_specs=in_specs, out_specs=out_specs, check_vma=False)
```

```python
import functools
import math

import jax
import jax.numpy as jnp
from jax import lax
from jax.experimental import pallas as pl
from jax.experimental.pallas import tpu as pltpu
from jax.sharding import PartitionSpec as P

BLOCK = 512
LANES = 128
DIM = 32
DEPTH = 112
PACK = 17
VMEM_LIMIT = 16 * 2**20

epsilon = 0.01
very_low = -1e30
log2e = math.log2(math.e)
unit = epsilon / log2e
cross_scale = 2.0 / (DIM * unit)
square_scale = 1.0 / (DIM * unit)

F32 = jnp.float32
BF16 = jnp.bfloat16


def pieces(vec):
    first = vec.astype(BF16).astype(F32)
    rest = vec - first
    second = rest.astype(BF16).astype(F32)
    return first, second, rest - second


def bias_rows(vec):
    row = lax.broadcasted_iota(jnp.int32, (16, vec.shape[1]), 0)
    a, b, c = pieces(vec)
    return jnp.where(row == 0, a, jnp.where(row == 1, b, jnp.where(row == 2, c, 0.0))).astype(BF16)


def one_rows(width):
    row = lax.broadcasted_iota(jnp.int32, (16, width), 0)
    return jnp.where(row < 3, 1.0, 0.0).astype(BF16)


def fill_src(x_ref, xs_ref):
    for b in range(xs_ref.shape[0]):
        xs = x_ref[:, b * BLOCK : (b + 1) * BLOCK].astype(F32) * cross_scale
        for k, piece in enumerate(pieces(xs)):
            xs_ref[b, k * DIM : (k + 1) * DIM, :] = piece.astype(BF16)


def src_operand(xs_ref, s, tail):
    return jnp.concatenate([xs_ref[s], tail], axis=0)


def tgt_block(y_ref, t):
    return y_ref[:, pl.ds(pl.multiple_of(t * BLOCK, BLOCK), BLOCK)]


def tgt_operand(y_ref, t, tail):
    block = tgt_block(y_ref, t)
    return jnp.concatenate([block, block, block, tail], axis=0)


def tile_scores(left, right):
    return lax.dot_general(left, right, (((0,), (0,)), ((), ())), preferred_element_type=F32)


CHUNK = 128


UNROLL = 4
BARY_UNROLL = 2


def tile_lse(left, right):
    top = total = None
    scores = tile_scores(left, right)
    for c in range(0, BLOCK, CHUNK):
        score = scores[c : c + CHUNK, :].reshape(CHUNK // 8, 8, BLOCK)
        most = jnp.max(score, axis=0)
        old, top = top, most if c == 0 else jnp.maximum(top, most)
        part = jnp.sum(jnp.exp2(score - top), axis=0)
        total = part if c == 0 else total * jnp.exp2(old - top) + part
    return top, total


def add_tile(tile, top_ref, total_ref, at):
    top, total = tile
    old = top_ref[at]
    most = jnp.maximum(old, top)
    total_ref[at] = total_ref[at] * jnp.exp2(old - most) + total * jnp.exp2(top - most)
    top_ref[at] = most


def lse_tiles(count, slots, left_of, right_of, at_of, spare, top_ref, total_ref):
    def step(q, carry):
        tiles = []
        for u in range(UNROLL):
            p = q * UNROLL + u
            live = p < count
            p = jnp.minimum(p, count - 1)
            s, t = slots[0, p], slots[1, p]
            tiles.append((tile_lse(left_of(s, t), right_of(s, t)), jnp.where(live, at_of(s, t), spare)))
        for tile, at in tiles:
            add_tile(tile, top_ref, total_ref, at)
        return carry

    lax.fori_loop(0, lax.div(count + UNROLL - 1, UNROLL), step, 0)


def joined(top, total):
    most = jnp.max(top, axis=0, keepdims=True)
    total = jnp.sum(total * jnp.exp2(top - most), axis=0, keepdims=True)
    return jnp.where(total > 0.0, most + jnp.log2(total), very_low)


def clear(top_ref, total_ref):
    top_ref[...] = jnp.full(top_ref.shape, very_low, F32)
    total_ref[...] = jnp.zeros(total_ref.shape, F32)


def spread_rows(blocks, top_ref, total_ref, out_ref, copies):
    per = BLOCK // LANES
    rows = blocks * per
    for b in range(blocks):
        lse = joined(top_ref[b], total_ref[b])
        for k in range(per):
            out_ref[b * per + k : b * per + k + 1, :] = lse[:, k * LANES : (k + 1) * LANES]
    value = out_ref[0:rows, :]
    for c in range(1, copies):
        out_ref[c * rows : (c + 1) * rows, :] = value


def merged(in_ref, parts):
    rows = in_ref.shape[0] // parts
    values = [in_ref[c * rows : (c + 1) * rows, :] for c in range(parts)]
    top = functools.reduce(jnp.maximum, values)
    total = functools.reduce(jnp.add, [jnp.exp2(v - top) for v in values])
    return top + jnp.log2(total)


def fetch(sources, targets, sems):
    copies = [
        pltpu.make_async_copy(source, target, sems.at[k])
        for k, (source, target) in enumerate(zip(sources, targets))
    ]
    for copy in copies:
        copy.start()
    return copies


def src_kernel(parts, count, slots_in, x_in, y_in, g_in, out_ref, xs_ref, slots, x_ref, y_ref, g_ref, sems, bias_ref, top_ref, total_ref):
    copies = fetch(
        (x_in, y_in, g_in, slots_in), (x_ref, y_ref, g_ref, slots), sems
    )
    clear(top_ref, total_ref)
    for copy in copies:
        copy.wait()
    fill_src(x_ref, xs_ref)
    for b in range(bias_ref.shape[0]):
        ys = y_ref[:, b * BLOCK : (b + 1) * BLOCK].astype(F32)
        square = jnp.sum(ys * ys, axis=0, keepdims=True)
        start = g_ref[:, b * BLOCK : (b + 1) * BLOCK]
        bias_ref[b] = bias_rows(start / unit - square * square_scale)
    ones = one_rows(BLOCK)
    blocks = xs_ref.shape[0]
    lse_tiles(
        count[0, 0],
        slots,
        lambda s, t: tgt_operand(y_ref, t, bias_ref[t]),
        lambda s, t: src_operand(xs_ref, s, ones),
        lambda s, t: s,
        blocks,
        top_ref,
        total_ref,
    )
    spread_rows(blocks, top_ref, total_ref, out_ref, parts)


def merge_kernel(parts, in_ref, out_ref):
    value = merged(in_ref, parts)
    rows = value.shape[0]
    for c in range(parts):
        out_ref[c * rows : (c + 1) * rows, :] = value


def tgt_kernel(parts, copies, log_rows, count, slots_in, in_ref, xs_ref, x_ref, y_ref, f_out, out_ref, slots, f_ref, sems, bias_ref, top_ref, total_ref):
    fetched = fetch((slots_in,), (slots,), sems)[0]
    clear(top_ref, total_ref)
    bias = -log_rows - merged(in_ref, parts)
    per = BLOCK // LANES
    for b in range(bias_ref.shape[0]):
        xs = x_ref[:, b * BLOCK : (b + 1) * BLOCK].astype(F32)
        square = jnp.sum(xs * xs, axis=0, keepdims=True)
        for k in range(per):
            row = b * per + k
            lanes = slice(k * LANES, (k + 1) * LANES)
            one = bias[row : row + 1, :]
            bias_ref[b, :, lanes] = bias_rows(one)
            f_ref[row : row + 1, :] = unit * one + square[:, lanes] * (1.0 / DIM)
    written = pltpu.make_async_copy(f_ref, f_out, sems.at[1])
    fetched.wait()
    written.start()
    ones = one_rows(BLOCK)
    blocks = y_ref.shape[1] // BLOCK
    lse_tiles(
        count[0, 0],
        slots,
        lambda s, t: src_operand(xs_ref, s, bias_ref[s]),
        lambda s, t: tgt_operand(y_ref, t, ones),
        lambda s, t: t,
        blocks,
        top_ref,
        total_ref,
    )
    spread_rows(blocks, top_ref, total_ref, out_ref, copies)
    written.wait()


def bary_kernel(parts, log_cols, count, slots_in, in_ref, xs_ref, y_ref, g_out, out_ref, slots, g_ref, sems, bias_ref, top_ref, acc_ref):
    fetched = fetch((slots_in,), (slots,), sems)[0]
    top_ref[...] = jnp.full(top_ref.shape, very_low, F32)
    acc_ref[...] = jnp.zeros(acc_ref.shape, F32)
    bias = -log_cols - merged(in_ref, parts)
    per = BLOCK // LANES
    for b in range(bias_ref.shape[0]):
        ys = y_ref[:, b * BLOCK : (b + 1) * BLOCK].astype(F32)
        square = jnp.sum(ys * ys, axis=0, keepdims=True)
        for k in range(per):
            row = b * per + k
            lanes = slice(k * LANES, (k + 1) * LANES)
            one = bias[row : row + 1, :]
            bias_ref[b, :, lanes] = bias_rows(one)
            g_ref[row : row + 1, :] = unit * one + square[:, lanes] * (1.0 / DIM)
    written = pltpu.make_async_copy(g_ref, g_out, sems.at[1])
    fetched.wait()
    written.start()
    spare = xs_ref.shape[0]
    ones = one_rows(BLOCK)
    first_row = lax.broadcasted_iota(jnp.int32, (16, BLOCK), 0) == 0
    total_row = jnp.where(first_row, 1.0, 0.0).astype(BF16)

    def step(q, carry):
        tiles = []
        for u in range(BARY_UNROLL):
            p = q * BARY_UNROLL + u
            live = p < count[0, 0]
            p = jnp.minimum(p, count[0, 0] - 1)
            s, t = slots[0, p], slots[1, p]
            scores = tile_scores(tgt_operand(y_ref, t, bias_ref[t]), src_operand(xs_ref, s, ones))
            values = jnp.concatenate([tgt_block(y_ref, t), total_row], axis=0)
            top = part = None
            for c in range(0, BLOCK, CHUNK):
                score = scores[c : c + CHUNK, :]
                most = jnp.max(score, axis=0, keepdims=True)
                old, top = top, most if c == 0 else jnp.maximum(top, most)
                weight = jnp.exp2(score - top).astype(BF16)
                more = jnp.dot(values[:, c : c + CHUNK], weight, preferred_element_type=F32)
                part = more if c == 0 else part * jnp.exp2(old - top) + more
            tiles.append((top, part, jnp.where(live, s, spare)))
        for top, part, at in tiles:
            old = top_ref[at]
            most = jnp.maximum(old, top)
            acc_ref[at] = acc_ref[at] * jnp.exp2(old - most) + part * jnp.exp2(top - most)
            top_ref[at] = most
        return carry

    lax.fori_loop(0, lax.div(count[0, 0] + BARY_UNROLL - 1, BARY_UNROLL), step, 0)
    for b in range(spare):
        total = acc_ref[b, 32:33, :]
        live = total > 0.0
        lse = jnp.where(live, top_ref[b] + jnp.log2(total), very_low)
        mean = acc_ref[b, 0:32, :] * jnp.where(live, 1.0 / total, 0.0)
        for k in range(per):
            lanes = slice(k * LANES, (k + 1) * LANES)
            for h in range(2):
                at = ((b * per + k) * 2 + h) * PACK
                out_ref[at : at + 16, :] = mean[h * 16 : h * 16 + 16, lanes]
                out_ref[at + 16 : at + 17, :] = lse[:, lanes]
    written.wait()

def mean_kernel(parts, in_ref, out_ref):
    logs = [in_ref[c * PACK + 16 : c * PACK + 17, :] for c in range(parts)]
    top = functools.reduce(jnp.maximum, logs)
    total = jnp.zeros_like(top)
    value = jnp.zeros((16, LANES), F32)
    for c in range(parts):
        weight = jnp.exp2(logs[c] - top)
        total = total + weight
        value = value + weight * in_ref[c * PACK : c * PACK + 16, :]
    value = value / total
    for c in range(parts):
        out_ref[c * 16 : (c + 1) * 16, :] = value


def place_kernel(in_ref, out_ref, sems):
    half = in_ref.shape[0] // 2
    copies = []
    for d in range(4):
        for k in range(2):
            runs = pl.ds(k * half, half)
            copies.append(
                pltpu.make_async_copy(
                    in_ref.at[runs, d // 2, d % 2], out_ref.at[d, runs], sems.at[2 * d + k]
                )
            )
    for copy in copies:
        copy.start()
    for copy in copies:
        copy.wait()


def whole(count):
    return [pl.BlockSpec(memory_space=pltpu.VMEM)] * count


def scalar():
    return pl.BlockSpec(memory_space=pltpu.SMEM)


def far():
    return pl.BlockSpec(memory_space=pltpu.HBM)


def body(src_latent, tgt_latent, g_start, pairs, counts):
    src_len = src_latent.shape[1]
    tgt_len = tgt_latent.shape[1]
    n_row, n_col = lax.axis_size("row"), lax.axis_size("col")
    side = 8
    other = n_col // side
    groups_z = [[z * side + y for z in range(other)] for y in range(side)]
    groups_y = [[z * side + y for y in range(side)] for z in range(other)]
    slots = pltpu.with_memory_space_constraint(pairs.reshape(pairs.shape[2:]).T, pltpu.HBM)
    count = counts
    s_blocks, t_blocks = src_len // BLOCK, tgt_len // BLOCK
    s_rows, t_rows = src_len // LANES, tgt_len // LANES
    log_rows = math.log2(src_len * n_row)
    log_cols = math.log2(tgt_len * n_col)

    def tails(blocks):
        return pltpu.VMEM((blocks, 16, BLOCK), BF16)

    def line(blocks, rows=8):
        return pltpu.VMEM((blocks, rows, BLOCK), F32)

    def side_refs(rows):
        return (
            pltpu.SMEM(slots.shape, jnp.int32),
            pltpu.VMEM((rows, LANES), F32),
            pltpu.SemaphoreType.DMA((2,)),
        )

    def exchange(x, axis, parts, groups=None):
        width = x.shape[0] // parts * LANES
        y = lax.all_to_all(
            x.reshape(parts, width), axis, 0, 0, axis_index_groups=groups, tiled=True
        )
        return y.reshape(-1, LANES)

    def rows_of(n):
        return jax.ShapeDtypeStruct((n, LANES), F32)

    lse, xs = pl.pallas_call(
        functools.partial(src_kernel, other),
        out_shape=(
            rows_of(other * s_rows),
            jax.ShapeDtypeStruct((s_blocks, 3 * DIM, BLOCK), BF16),
        ),
        in_specs=[scalar()] + [far()] * 4,
        out_specs=tuple(whole(2)),
        scratch_shapes=[
            pltpu.SMEM(slots.shape, jnp.int32),
            pltpu.VMEM(src_latent.shape, BF16),
            pltpu.VMEM(tgt_latent.shape, BF16),
            pltpu.VMEM((1, tgt_len), F32),
            pltpu.SemaphoreType.DMA((4,)),
            tails(t_blocks), line(s_blocks + 1), line(s_blocks + 1)],
        compiler_params=pltpu.CompilerParams(vmem_limit_bytes=VMEM_LIMIT),
        name="src_pass",
    )(count, slots, *[
        pltpu.with_memory_space_constraint(a, pltpu.HBM)
        for a in (src_latent, tgt_latent, g_start.reshape(1, -1))
    ])
    lse = exchange(lse, "col", other, groups_z)
    lse = pl.pallas_call(
        functools.partial(merge_kernel, other),
        out_shape=rows_of(side * s_rows),
        in_specs=whole(1),
        out_specs=whole(1)[0],
        compiler_params=pltpu.CompilerParams(vmem_limit_bytes=VMEM_LIMIT),
        name="src_merge",
    )(lse)
    lse = exchange(lse, "col", side, groups_y)
    f_new, lse = pl.pallas_call(
        functools.partial(tgt_kernel, side, n_row, log_rows),
        out_shape=(rows_of(s_rows), rows_of(n_row * t_rows)),
        in_specs=[scalar(), far()] + whole(4),
        out_specs=(far(), whole(1)[0]),
        scratch_shapes=[*side_refs(s_rows), tails(s_blocks), line(t_blocks + 1), line(t_blocks + 1)],
        compiler_params=pltpu.CompilerParams(vmem_limit_bytes=VMEM_LIMIT),
        name="tgt_pass",
    )(count, slots, lse, xs, src_latent, tgt_latent)
    lse = exchange(lse, "row", n_row)
    g_new, means = pl.pallas_call(
        functools.partial(bary_kernel, n_row, log_cols),
        out_shape=(rows_of(t_rows), rows_of(n_col * PACK)),
        in_specs=[scalar(), far()] + whole(3),
        out_specs=(far(), whole(1)[0]),
        scratch_shapes=[
            *side_refs(t_rows),
            tails(t_blocks),
            line(s_blocks + 1, 1),
            pltpu.VMEM((s_blocks + 1, 48, BLOCK), F32),
        ],
        compiler_params=pltpu.CompilerParams(vmem_limit_bytes=VMEM_LIMIT),
        name="bary_pass",
    )(count, slots, lse, xs, tgt_latent)
    means = exchange(means, "col", n_col)
    means = pl.pallas_call(
        functools.partial(mean_kernel, n_col),
        out_shape=rows_of(n_col * 16),
        in_specs=whole(1),
        out_specs=whole(1)[0],
        compiler_params=pltpu.CompilerParams(vmem_limit_bytes=VMEM_LIMIT),
        name="bary_merge",
    )(means)
    means = exchange(means, "col", n_col)
    tiles = pl.pallas_call(
        place_kernel,
        out_shape=jax.ShapeDtypeStruct((DIM // 8, s_rows, 8, LANES), F32),
        in_specs=whole(1),
        out_specs=far(),
        scratch_shapes=[pltpu.SemaphoreType.DMA((8,))],
        compiler_params=pltpu.CompilerParams(vmem_limit_bytes=VMEM_LIMIT),
        name="bary_place",
    )(means.reshape(s_rows, 2, 2, 8, LANES))
    bary = tiles.transpose(0, 2, 1, 3).reshape(DIM, src_len)
    return f_new.reshape(-1), g_new.reshape(-1), bary


def solution(mesh):
    in_specs = (
        P(None, "row"),
        P(None, "col"),
        P("col"),
        P("row", "col", None, None),
        P("row", "col"),
    )
    out_specs = (P("row"), P("col"), P(None, "row"))
    return jax.shard_map(body, mesh=mesh, in_specs=in_specs, out_specs=out_specs, check_vma=False)
```

```python
import functools
import math

import jax
import jax.numpy as jnp
from jax import lax
from jax.experimental import pallas as pl
from jax.experimental.pallas import tpu as pltpu
from jax.sharding import PartitionSpec as P

BLOCK = 512
LANES = 128
DIM = 32
DEPTH = 112
PACK = 17
LATE = 0
HOLD = 5000
VMEM_LIMIT = 16 * 2**20

epsilon = 0.01
very_low = -1e30
log2e = math.log2(math.e)
unit = epsilon / log2e
cross_scale = 2.0 / (DIM * unit)
square_scale = 1.0 / (DIM * unit)

F32 = jnp.float32
BF16 = jnp.bfloat16


def pieces(vec):
    first = vec.astype(BF16).astype(F32)
    rest = vec - first
    second = rest.astype(BF16).astype(F32)
    return first, second, rest - second


def bias_rows(vec):
    row = lax.broadcasted_iota(jnp.int32, (16, vec.shape[1]), 0)
    a, b, c = pieces(vec)
    return jnp.where(row == 0, a, jnp.where(row == 1, b, jnp.where(row == 2, c, 0.0))).astype(BF16)


def one_rows(width):
    row = lax.broadcasted_iota(jnp.int32, (16, width), 0)
    return jnp.where(row < 3, 1.0, 0.0).astype(BF16)


def fill_src(x_ref, xs_ref):
    for b in range(xs_ref.shape[0]):
        xs = x_ref[:, b * BLOCK : (b + 1) * BLOCK].astype(F32) * cross_scale
        for k, piece in enumerate(pieces(xs)):
            xs_ref[b, k * DIM : (k + 1) * DIM, :] = piece.astype(BF16)


def src_operand(xs_ref, s, tail):
    return jnp.concatenate([xs_ref[s], tail], axis=0)


def tgt_block(y_ref, t):
    return y_ref[:, pl.ds(pl.multiple_of(t * BLOCK, BLOCK), BLOCK)]


def tgt_operand(y_ref, t, tail):
    block = tgt_block(y_ref, t)
    return jnp.concatenate([block, block, block, tail], axis=0)


def tile_scores(left, right):
    return lax.dot_general(left, right, (((0,), (0,)), ((), ())), preferred_element_type=F32)


CHUNK = 128


UNROLL = 4
BARY_UNROLL = 2


def tile_lse(left, right):
    top = total = None
    scores = tile_scores(left, right)
    for c in range(0, BLOCK, CHUNK):
        score = scores[c : c + CHUNK, :].reshape(CHUNK // 8, 8, BLOCK)
        most = jnp.max(score, axis=0)
        old, top = top, most if c == 0 else jnp.maximum(top, most)
        part = jnp.sum(jnp.exp2(score - top), axis=0)
        total = part if c == 0 else total * jnp.exp2(old - top) + part
    return top, total


def add_tile(tile, top_ref, total_ref, at):
    top, total = tile
    old = top_ref[at]
    most = jnp.maximum(old, top)
    total_ref[at] = total_ref[at] * jnp.exp2(old - most) + total * jnp.exp2(top - most)
    top_ref[at] = most


def lse_tiles(count, slots, left_of, right_of, at_of, spare, top_ref, total_ref):
    def step(q, carry):
        tiles = []
        for u in range(UNROLL):
            p = q * UNROLL + u
            live = p < count
            p = jnp.minimum(p, count - 1)
            s, t = slots[0, p], slots[1, p]
            tiles.append((tile_lse(left_of(s, t), right_of(s, t)), jnp.where(live, at_of(s, t), spare)))
        for tile, at in tiles:
            add_tile(tile, top_ref, total_ref, at)
        return carry

    lax.fori_loop(0, lax.div(count + UNROLL - 1, UNROLL), step, 0)


def joined(top, total):
    most = jnp.max(top, axis=0, keepdims=True)
    total = jnp.sum(total * jnp.exp2(top - most), axis=0, keepdims=True)
    return jnp.where(total > 0.0, most + jnp.log2(total), very_low)


def clear(top_ref, total_ref):
    top_ref[...] = jnp.full(top_ref.shape, very_low, F32)
    total_ref[...] = jnp.zeros(total_ref.shape, F32)


def spread_rows(blocks, top_ref, total_ref, out_ref, copies):
    per = BLOCK // LANES
    rows = blocks * per
    for b in range(blocks):
        lse = joined(top_ref[b], total_ref[b])
        for k in range(per):
            out_ref[b * per + k : b * per + k + 1, :] = lse[:, k * LANES : (k + 1) * LANES]
    value = out_ref[0:rows, :]
    for c in range(1, copies):
        out_ref[c * rows : (c + 1) * rows, :] = value


def merged(in_ref, parts):
    rows = in_ref.shape[0] // parts
    values = [in_ref[c * rows : (c + 1) * rows, :] for c in range(parts)]
    top = functools.reduce(jnp.maximum, values)
    total = functools.reduce(jnp.add, [jnp.exp2(v - top) for v in values])
    return top + jnp.log2(total)


def fetch(sources, targets, sems):
    copies = [
        pltpu.make_async_copy(source, target, sems.at[k])
        for k, (source, target) in enumerate(zip(sources, targets))
    ]
    for copy in copies:
        copy.start()
    return copies


def src_kernel(parts, count, slots_in, x_in, y_in, g_in, out_ref, xs_ref, slots, x_ref, y_ref, g_ref, sems, bias_ref, top_ref, total_ref):
    copies = fetch(
        (x_in, y_in, g_in, slots_in), (x_ref, y_ref, g_ref, slots), sems
    )
    clear(top_ref, total_ref)
    for copy in copies:
        copy.wait()
    fill_src(x_ref, xs_ref)
    for b in range(bias_ref.shape[0]):
        ys = y_ref[:, b * BLOCK : (b + 1) * BLOCK].astype(F32)
        square = jnp.sum(ys * ys, axis=0, keepdims=True)
        start = g_ref[:, b * BLOCK : (b + 1) * BLOCK]
        bias_ref[b] = bias_rows(start / unit - square * square_scale)
    ones = one_rows(BLOCK)
    blocks = xs_ref.shape[0]
    lse_tiles(
        count[0, 0],
        slots,
        lambda s, t: tgt_operand(y_ref, t, bias_ref[t]),
        lambda s, t: src_operand(xs_ref, s, ones),
        lambda s, t: s,
        blocks,
        top_ref,
        total_ref,
    )
    spread_rows(blocks, top_ref, total_ref, out_ref, parts)


def merge_kernel(parts, in_ref, out_ref):
    value = merged(in_ref, parts)
    rows = value.shape[0]
    for c in range(parts):
        out_ref[c * rows : (c + 1) * rows, :] = value


def tgt_kernel(parts, copies, log_rows, count, slots_in, in_ref, xs_ref, x_ref, y_ref, f_out, out_ref, slots, f_ref, sems, bias_ref, top_ref, total_ref):
    fetched = fetch((slots_in,), (slots,), sems)[0]
    clear(top_ref, total_ref)
    bias = -log_rows - merged(in_ref, parts)
    per = BLOCK // LANES
    for b in range(bias_ref.shape[0]):
        xs = x_ref[:, b * BLOCK : (b + 1) * BLOCK].astype(F32)
        square = jnp.sum(xs * xs, axis=0, keepdims=True)
        for k in range(per):
            row = b * per + k
            lanes = slice(k * LANES, (k + 1) * LANES)
            one = bias[row : row + 1, :]
            bias_ref[b, :, lanes] = bias_rows(one)
            f_ref[row : row + 1, :] = unit * one + square[:, lanes] * (1.0 / DIM)
    written = pltpu.make_async_copy(f_ref, f_out, sems.at[1])
    fetched.wait()
    written.start()
    ones = one_rows(BLOCK)
    blocks = y_ref.shape[1] // BLOCK
    lse_tiles(
        count[0, 0],
        slots,
        lambda s, t: src_operand(xs_ref, s, bias_ref[s]),
        lambda s, t: tgt_operand(y_ref, t, ones),
        lambda s, t: t,
        blocks,
        top_ref,
        total_ref,
    )
    spread_rows(blocks, top_ref, total_ref, out_ref, copies)
    written.wait()


def bary_kernel(parts, log_cols, count, slots_in, in_ref, xs_ref, y_ref, g_out, out_ref, slots, g_ref, sems, bias_ref, top_ref, acc_ref):
    fetched = fetch((slots_in,), (slots,), sems)[0]
    top_ref[...] = jnp.full(top_ref.shape, very_low, F32)
    acc_ref[...] = jnp.zeros(acc_ref.shape, F32)
    bias = -log_cols - merged(in_ref, parts)
    per = BLOCK // LANES
    for b in range(bias_ref.shape[0]):
        ys = y_ref[:, b * BLOCK : (b + 1) * BLOCK].astype(F32)
        square = jnp.sum(ys * ys, axis=0, keepdims=True)
        for k in range(per):
            row = b * per + k
            lanes = slice(k * LANES, (k + 1) * LANES)
            one = bias[row : row + 1, :]
            bias_ref[b, :, lanes] = bias_rows(one)
            g_ref[row : row + 1, :] = unit * one + square[:, lanes] * (1.0 / DIM)
    written = pltpu.make_async_copy(g_ref, g_out, sems.at[1])
    fetched.wait()
    written.start()

    @pl.when(lax.rem(lax.axis_index("row"), 2) == LATE)
    def _():
        pl.delay(HOLD)

    spare = xs_ref.shape[0]
    ones = one_rows(BLOCK)
    first_row = lax.broadcasted_iota(jnp.int32, (16, BLOCK), 0) == 0
    total_row = jnp.where(first_row, 1.0, 0.0).astype(BF16)

    def step(q, carry):
        tiles = []
        for u in range(BARY_UNROLL):
            p = q * BARY_UNROLL + u
            live = p < count[0, 0]
            p = jnp.minimum(p, count[0, 0] - 1)
            s, t = slots[0, p], slots[1, p]
            scores = tile_scores(tgt_operand(y_ref, t, bias_ref[t]), src_operand(xs_ref, s, ones))
            values = jnp.concatenate([tgt_block(y_ref, t), total_row], axis=0)
            top = part = None
            for c in range(0, BLOCK, CHUNK):
                score = scores[c : c + CHUNK, :]
                most = jnp.max(score, axis=0, keepdims=True)
                old, top = top, most if c == 0 else jnp.maximum(top, most)
                weight = jnp.exp2(score - top).astype(BF16)
                more = jnp.dot(values[:, c : c + CHUNK], weight, preferred_element_type=F32)
                part = more if c == 0 else part * jnp.exp2(old - top) + more
            tiles.append((top, part, jnp.where(live, s, spare)))
        for top, part, at in tiles:
            old = top_ref[at]
            most = jnp.maximum(old, top)
            acc_ref[at] = acc_ref[at] * jnp.exp2(old - most) + part * jnp.exp2(top - most)
            top_ref[at] = most
        return carry

    lax.fori_loop(0, lax.div(count[0, 0] + BARY_UNROLL - 1, BARY_UNROLL), step, 0)
    for b in range(spare):
        total = acc_ref[b, 32:33, :]
        live = total > 0.0
        lse = jnp.where(live, top_ref[b] + jnp.log2(total), very_low)
        mean = acc_ref[b, 0:32, :] * jnp.where(live, 1.0 / total, 0.0)
        for k in range(per):
            lanes = slice(k * LANES, (k + 1) * LANES)
            for h in range(2):
                at = ((b * per + k) * 2 + h) * PACK
                out_ref[at : at + 16, :] = mean[h * 16 : h * 16 + 16, lanes]
                out_ref[at + 16 : at + 17, :] = lse[:, lanes]
    written.wait()

def mean_kernel(parts, in_ref, out_ref):
    logs = [in_ref[c * PACK + 16 : c * PACK + 17, :] for c in range(parts)]
    top = functools.reduce(jnp.maximum, logs)
    total = jnp.zeros_like(top)
    value = jnp.zeros((16, LANES), F32)
    for c in range(parts):
        weight = jnp.exp2(logs[c] - top)
        total = total + weight
        value = value + weight * in_ref[c * PACK : c * PACK + 16, :]
    value = value / total
    for c in range(parts):
        out_ref[c * 16 : (c + 1) * 16, :] = value


def place_kernel(in_ref, out_ref, sems):
    half = in_ref.shape[0] // 2
    copies = []
    for d in range(4):
        for k in range(2):
            runs = pl.ds(k * half, half)
            copies.append(
                pltpu.make_async_copy(
                    in_ref.at[runs, d // 2, d % 2], out_ref.at[d, runs], sems.at[2 * d + k]
                )
            )
    for copy in copies:
        copy.start()
    for copy in copies:
        copy.wait()


def whole(count):
    return [pl.BlockSpec(memory_space=pltpu.VMEM)] * count


def scalar():
    return pl.BlockSpec(memory_space=pltpu.SMEM)


def far():
    return pl.BlockSpec(memory_space=pltpu.HBM)


def body(src_latent, tgt_latent, g_start, pairs, counts):
    src_len = src_latent.shape[1]
    tgt_len = tgt_latent.shape[1]
    n_row, n_col = lax.axis_size("row"), lax.axis_size("col")
    side = 8
    other = n_col // side
    groups_z = [[z * side + y for z in range(other)] for y in range(side)]
    groups_y = [[z * side + y for y in range(side)] for z in range(other)]
    slots = pltpu.with_memory_space_constraint(pairs.reshape(pairs.shape[2:]).T, pltpu.HBM)
    count = counts
    s_blocks, t_blocks = src_len // BLOCK, tgt_len // BLOCK
    s_rows, t_rows = src_len // LANES, tgt_len // LANES
    log_rows = math.log2(src_len * n_row)
    log_cols = math.log2(tgt_len * n_col)

    def tails(blocks):
        return pltpu.VMEM((blocks, 16, BLOCK), BF16)

    def line(blocks, rows=8):
        return pltpu.VMEM((blocks, rows, BLOCK), F32)

    def side_refs(rows):
        return (
            pltpu.SMEM(slots.shape, jnp.int32),
            pltpu.VMEM((rows, LANES), F32),
            pltpu.SemaphoreType.DMA((2,)),
        )

    def exchange(x, axis, parts, groups=None):
        width = x.shape[0] // parts * LANES
        y = lax.all_to_all(
            x.reshape(parts, width), axis, 0, 0, axis_index_groups=groups, tiled=True
        )
        return y.reshape(-1, LANES)

    def rows_of(n):
        return jax.ShapeDtypeStruct((n, LANES), F32)

    lse, xs = pl.pallas_call(
        functools.partial(src_kernel, other),
        out_shape=(
            rows_of(other * s_rows),
            jax.ShapeDtypeStruct((s_blocks, 3 * DIM, BLOCK), BF16),
        ),
        in_specs=[scalar()] + [far()] * 4,
        out_specs=tuple(whole(2)),
        scratch_shapes=[
            pltpu.SMEM(slots.shape, jnp.int32),
            pltpu.VMEM(src_latent.shape, BF16),
            pltpu.VMEM(tgt_latent.shape, BF16),
            pltpu.VMEM((1, tgt_len), F32),
            pltpu.SemaphoreType.DMA((4,)),
            tails(t_blocks), line(s_blocks + 1), line(s_blocks + 1)],
        compiler_params=pltpu.CompilerParams(vmem_limit_bytes=VMEM_LIMIT),
        name="src_pass",
    )(count, slots, *[
        pltpu.with_memory_space_constraint(a, pltpu.HBM)
        for a in (src_latent, tgt_latent, g_start.reshape(1, -1))
    ])
    lse = exchange(lse, "col", other, groups_z)
    lse = pl.pallas_call(
        functools.partial(merge_kernel, other),
        out_shape=rows_of(side * s_rows),
        in_specs=whole(1),
        out_specs=whole(1)[0],
        compiler_params=pltpu.CompilerParams(vmem_limit_bytes=VMEM_LIMIT),
        name="src_merge",
    )(lse)
    lse = exchange(lse, "col", side, groups_y)
    f_new, lse = pl.pallas_call(
        functools.partial(tgt_kernel, side, n_row, log_rows),
        out_shape=(rows_of(s_rows), rows_of(n_row * t_rows)),
        in_specs=[scalar(), far()] + whole(4),
        out_specs=(far(), whole(1)[0]),
        scratch_shapes=[*side_refs(s_rows), tails(s_blocks), line(t_blocks + 1), line(t_blocks + 1)],
        compiler_params=pltpu.CompilerParams(vmem_limit_bytes=VMEM_LIMIT),
        name="tgt_pass",
    )(count, slots, lse, xs, src_latent, tgt_latent)
    lse = exchange(lse, "row", n_row)
    g_new, means = pl.pallas_call(
        functools.partial(bary_kernel, n_row, log_cols),
        out_shape=(rows_of(t_rows), rows_of(n_col * PACK)),
        in_specs=[scalar(), far()] + whole(3),
        out_specs=(far(), whole(1)[0]),
        scratch_shapes=[
            *side_refs(t_rows),
            tails(t_blocks),
            line(s_blocks + 1, 1),
            pltpu.VMEM((s_blocks + 1, 48, BLOCK), F32),
        ],
        compiler_params=pltpu.CompilerParams(vmem_limit_bytes=VMEM_LIMIT),
        name="bary_pass",
    )(count, slots, lse, xs, tgt_latent)
    means = exchange(means, "col", n_col)
    means = pl.pallas_call(
        functools.partial(mean_kernel, n_col),
        out_shape=rows_of(n_col * 16),
        in_specs=whole(1),
        out_specs=whole(1)[0],
        compiler_params=pltpu.CompilerParams(vmem_limit_bytes=VMEM_LIMIT),
        name="bary_merge",
    )(means)
    means = exchange(means, "col", n_col)
    tiles = pl.pallas_call(
        place_kernel,
        out_shape=jax.ShapeDtypeStruct((DIM // 8, s_rows, 8, LANES), F32),
        in_specs=whole(1),
        out_specs=far(),
        scratch_shapes=[pltpu.SemaphoreType.DMA((8,))],
        compiler_params=pltpu.CompilerParams(vmem_limit_bytes=VMEM_LIMIT),
        name="bary_place",
    )(means.reshape(s_rows, 2, 2, 8, LANES))
    bary = tiles.transpose(0, 2, 1, 3).reshape(DIM, src_len)
    return f_new.reshape(-1), g_new.reshape(-1), bary


def solution(mesh):
    in_specs = (
        P(None, "row"),
        P(None, "col"),
        P("col"),
        P("row", "col", None, None),
        P("row", "col"),
    )
    out_specs = (P("row"), P("col"), P(None, "row"))
    return jax.shard_map(body, mesh=mesh, in_specs=in_specs, out_specs=out_specs, check_vma=False)
```

```python
import functools
import math

import jax
import jax.numpy as jnp
from jax import lax
from jax.experimental import pallas as pl
from jax.experimental.pallas import tpu as pltpu
from jax.sharding import PartitionSpec as P

BLOCK = 512
LANES = 128
DIM = 32
DEPTH = 112
PACK = 17
LATE = 0
HOLD = 5000
VMEM_LIMIT = 16 * 2**20

epsilon = 0.01
very_low = -1e30
log2e = math.log2(math.e)
unit = epsilon / log2e
cross_scale = 2.0 / (DIM * unit)
square_scale = 1.0 / (DIM * unit)

F32 = jnp.float32
BF16 = jnp.bfloat16


def pieces(vec):
    first = vec.astype(BF16).astype(F32)
    rest = vec - first
    second = rest.astype(BF16).astype(F32)
    return first, second, rest - second


def bias_rows(vec):
    row = lax.broadcasted_iota(jnp.int32, (16, vec.shape[1]), 0)
    a, b, c = pieces(vec)
    return jnp.where(row == 0, a, jnp.where(row == 1, b, jnp.where(row == 2, c, 0.0))).astype(BF16)


def one_rows(width):
    row = lax.broadcasted_iota(jnp.int32, (16, width), 0)
    return jnp.where(row < 3, 1.0, 0.0).astype(BF16)


def fill_src(x_ref, xs_ref):
    for b in range(xs_ref.shape[0]):
        xs = x_ref[:, b * BLOCK : (b + 1) * BLOCK].astype(F32) * cross_scale
        for k, piece in enumerate(pieces(xs)):
            xs_ref[b, k * DIM : (k + 1) * DIM, :] = piece.astype(BF16)


def src_operand(xs_ref, s, tail):
    return jnp.concatenate([xs_ref[s], tail], axis=0)


def tgt_block(y_ref, t):
    return y_ref[:, pl.ds(pl.multiple_of(t * BLOCK, BLOCK), BLOCK)]


def tgt_operand(y_ref, t, tail):
    block = tgt_block(y_ref, t)
    return jnp.concatenate([block, block, block, tail], axis=0)


def tile_scores(left, right):
    return lax.dot_general(left, right, (((0,), (0,)), ((), ())), preferred_element_type=F32)


CHUNK = 128


UNROLL = 4
BARY_UNROLL = 2


def tile_lse(left, right):
    top = total = None
    scores = tile_scores(left, right)
    for c in range(0, BLOCK, CHUNK):
        score = scores[c : c + CHUNK, :].reshape(CHUNK // 8, 8, BLOCK)
        most = jnp.max(score, axis=0)
        old, top = top, most if c == 0 else jnp.maximum(top, most)
        part = jnp.sum(jnp.exp2(score - top), axis=0)
        total = part if c == 0 else total * jnp.exp2(old - top) + part
    return top, total


def add_tile(tile, top_ref, total_ref, at):
    top, total = tile
    old = top_ref[at]
    most = jnp.maximum(old, top)
    total_ref[at] = total_ref[at] * jnp.exp2(old - most) + total * jnp.exp2(top - most)
    top_ref[at] = most


def lse_tiles(count, slots, left_of, right_of, at_of, spare, top_ref, total_ref):
    def step(q, carry):
        tiles = []
        for u in range(UNROLL):
            p = q * UNROLL + u
            live = p < count
            p = jnp.minimum(p, count - 1)
            s, t = slots[0, p], slots[1, p]
            tiles.append((tile_lse(left_of(s, t), right_of(s, t)), jnp.where(live, at_of(s, t), spare)))
        for tile, at in tiles:
            add_tile(tile, top_ref, total_ref, at)
        return carry

    lax.fori_loop(0, lax.div(count + UNROLL - 1, UNROLL), step, 0)


def joined(top, total):
    most = jnp.max(top, axis=0, keepdims=True)
    total = jnp.sum(total * jnp.exp2(top - most), axis=0, keepdims=True)
    return jnp.where(total > 0.0, most + jnp.log2(total), very_low)


def clear(top_ref, total_ref):
    top_ref[...] = jnp.full(top_ref.shape, very_low, F32)
    total_ref[...] = jnp.zeros(total_ref.shape, F32)


def spread_rows(blocks, top_ref, total_ref, out_ref, copies):
    per = BLOCK // LANES
    rows = blocks * per
    for b in range(blocks):
        lse = joined(top_ref[b], total_ref[b])
        for k in range(per):
            out_ref[b * per + k : b * per + k + 1, :] = lse[:, k * LANES : (k + 1) * LANES]
    value = out_ref[0:rows, :]
    for c in range(1, copies):
        out_ref[c * rows : (c + 1) * rows, :] = value


def merged(in_ref, parts):
    rows = in_ref.shape[0] // parts
    values = [in_ref[c * rows : (c + 1) * rows, :] for c in range(parts)]
    top = functools.reduce(jnp.maximum, values)
    total = functools.reduce(jnp.add, [jnp.exp2(v - top) for v in values])
    return top + jnp.log2(total)


def fetch(sources, targets, sems):
    copies = [
        pltpu.make_async_copy(source, target, sems.at[k])
        for k, (source, target) in enumerate(zip(sources, targets))
    ]
    for copy in copies:
        copy.start()
    return copies


def src_kernel(parts, count, slots_in, x_in, y_in, g_in, out_ref, xs_ref, slots, x_ref, y_ref, g_ref, sems, bias_ref, top_ref, total_ref):
    copies = fetch(
        (x_in, y_in, g_in, slots_in), (x_ref, y_ref, g_ref, slots), sems
    )
    clear(top_ref, total_ref)
    for copy in copies:
        copy.wait()
    fill_src(x_ref, xs_ref)
    for b in range(bias_ref.shape[0]):
        ys = y_ref[:, b * BLOCK : (b + 1) * BLOCK].astype(F32)
        square = jnp.sum(ys * ys, axis=0, keepdims=True)
        start = g_ref[:, b * BLOCK : (b + 1) * BLOCK]
        bias_ref[b] = bias_rows(start / unit - square * square_scale)
    ones = one_rows(BLOCK)
    blocks = xs_ref.shape[0]
    lse_tiles(
        count[0, 0],
        slots,
        lambda s, t: tgt_operand(y_ref, t, bias_ref[t]),
        lambda s, t: src_operand(xs_ref, s, ones),
        lambda s, t: s,
        blocks,
        top_ref,
        total_ref,
    )
    spread_rows(blocks, top_ref, total_ref, out_ref, parts)


def merge_kernel(parts, in_ref, out_ref):
    value = merged(in_ref, parts)
    rows = value.shape[0]
    for c in range(parts):
        out_ref[c * rows : (c + 1) * rows, :] = value


def tgt_kernel(parts, copies, log_rows, count, slots_in, in_ref, xs_ref, x_ref, y_ref, f_out, out_ref, slots, f_ref, sems, bias_ref, top_ref, total_ref):
    fetched = fetch((slots_in,), (slots,), sems)[0]
    clear(top_ref, total_ref)
    bias = -log_rows - merged(in_ref, parts)
    per = BLOCK // LANES
    for b in range(bias_ref.shape[0]):
        xs = x_ref[:, b * BLOCK : (b + 1) * BLOCK].astype(F32)
        square = jnp.sum(xs * xs, axis=0, keepdims=True)
        for k in range(per):
            row = b * per + k
            lanes = slice(k * LANES, (k + 1) * LANES)
            one = bias[row : row + 1, :]
            bias_ref[b, :, lanes] = bias_rows(one)
            f_ref[row : row + 1, :] = unit * one + square[:, lanes] * (1.0 / DIM)
    written = pltpu.make_async_copy(f_ref, f_out, sems.at[1])
    fetched.wait()
    written.start()
    ones = one_rows(BLOCK)
    blocks = y_ref.shape[1] // BLOCK
    lse_tiles(
        count[0, 0],
        slots,
        lambda s, t: src_operand(xs_ref, s, bias_ref[s]),
        lambda s, t: tgt_operand(y_ref, t, ones),
        lambda s, t: t,
        blocks,
        top_ref,
        total_ref,
    )
    spread_rows(blocks, top_ref, total_ref, out_ref, copies)
    written.wait()


def bary_kernel(parts, log_cols, count, slots_in, in_ref, xs_ref, y_ref, g_out, out_ref, slots, g_ref, sems, bias_ref, top_ref, acc_ref):
    fetched = fetch((slots_in,), (slots,), sems)[0]
    top_ref[...] = jnp.full(top_ref.shape, very_low, F32)
    acc_ref[...] = jnp.zeros(acc_ref.shape, F32)
    bias = -log_cols - merged(in_ref, parts)
    per = BLOCK // LANES
    for b in range(bias_ref.shape[0]):
        ys = y_ref[:, b * BLOCK : (b + 1) * BLOCK].astype(F32)
        square = jnp.sum(ys * ys, axis=0, keepdims=True)
        for k in range(per):
            row = b * per + k
            lanes = slice(k * LANES, (k + 1) * LANES)
            one = bias[row : row + 1, :]
            bias_ref[b, :, lanes] = bias_rows(one)
            g_ref[row : row + 1, :] = unit * one + square[:, lanes] * (1.0 / DIM)
    written = pltpu.make_async_copy(g_ref, g_out, sems.at[1])
    fetched.wait()
    written.start()

    @pl.when(lax.rem(lax.axis_index("row"), 2) == LATE)
    def _():
        pl.delay(HOLD)

    spare = xs_ref.shape[0]
    ones = one_rows(BLOCK)
    first_row = lax.broadcasted_iota(jnp.int32, (16, BLOCK), 0) == 0
    total_row = jnp.where(first_row, 1.0, 0.0).astype(BF16)

    def step(q, carry):
        work = []
        for u in range(BARY_UNROLL):
            p = q * BARY_UNROLL + u
            live = p < count[0, 0]
            p = jnp.minimum(p, count[0, 0] - 1)
            s, t = slots[0, p], slots[1, p]
            scores = tile_scores(tgt_operand(y_ref, t, bias_ref[t]), src_operand(xs_ref, s, ones))
            values = jnp.concatenate([tgt_block(y_ref, t), total_row], axis=0)
            work.append([scores, values, None, None, jnp.where(live, s, spare)])
        for item in work:
            for c in range(0, BLOCK, CHUNK):
                scores, values, top, part, at = item
                score = scores[c : c + CHUNK, :]
                most = jnp.max(score, axis=0, keepdims=True)
                old, top = top, most if c == 0 else jnp.maximum(top, most)
                weight = jnp.exp2(score - top).astype(BF16)
                more = jnp.dot(values[:, c : c + CHUNK], weight, preferred_element_type=F32)
                part = more if c == 0 else part * jnp.exp2(old - top) + more
                item[2:4] = top, part
        tiles = [item[2:] for item in work]
        for top, part, at in tiles:
            old = top_ref[at]
            most = jnp.maximum(old, top)
            acc_ref[at] = acc_ref[at] * jnp.exp2(old - most) + part * jnp.exp2(top - most)
            top_ref[at] = most
        return carry

    lax.fori_loop(0, lax.div(count[0, 0] + BARY_UNROLL - 1, BARY_UNROLL), step, 0)
    for b in range(spare):
        total = acc_ref[b, 32:33, :]
        live = total > 0.0
        lse = jnp.where(live, top_ref[b] + jnp.log2(total), very_low)
        mean = acc_ref[b, 0:32, :] * jnp.where(live, 1.0 / total, 0.0)
        for k in range(per):
            lanes = slice(k * LANES, (k + 1) * LANES)
            for h in range(2):
                at = ((b * per + k) * 2 + h) * PACK
                out_ref[at : at + 16, :] = mean[h * 16 : h * 16 + 16, lanes]
                out_ref[at + 16 : at + 17, :] = lse[:, lanes]
    written.wait()

def mean_kernel(parts, in_ref, out_ref):
    logs = [in_ref[c * PACK + 16 : c * PACK + 17, :] for c in range(parts)]
    top = functools.reduce(jnp.maximum, logs)
    total = jnp.zeros_like(top)
    value = jnp.zeros((16, LANES), F32)
    for c in range(parts):
        weight = jnp.exp2(logs[c] - top)
        total = total + weight
        value = value + weight * in_ref[c * PACK : c * PACK + 16, :]
    value = value / total
    for c in range(parts):
        out_ref[c * 16 : (c + 1) * 16, :] = value


def place_kernel(in_ref, out_ref, sems):
    half = in_ref.shape[0] // 2
    copies = []
    for d in range(4):
        for k in range(2):
            runs = pl.ds(k * half, half)
            copies.append(
                pltpu.make_async_copy(
                    in_ref.at[runs, d // 2, d % 2], out_ref.at[d, runs], sems.at[2 * d + k]
                )
            )
    for copy in copies:
        copy.start()
    for copy in copies:
        copy.wait()


def whole(count):
    return [pl.BlockSpec(memory_space=pltpu.VMEM)] * count


def scalar():
    return pl.BlockSpec(memory_space=pltpu.SMEM)


def far():
    return pl.BlockSpec(memory_space=pltpu.HBM)


def body(src_latent, tgt_latent, g_start, pairs, counts):
    src_len = src_latent.shape[1]
    tgt_len = tgt_latent.shape[1]
    n_row, n_col = lax.axis_size("row"), lax.axis_size("col")
    side = 8
    other = n_col // side
    groups_z = [[z * side + y for z in range(other)] for y in range(side)]
    groups_y = [[z * side + y for y in range(side)] for z in range(other)]
    slots = pltpu.with_memory_space_constraint(pairs.reshape(pairs.shape[2:]).T, pltpu.HBM)
    count = counts
    s_blocks, t_blocks = src_len // BLOCK, tgt_len // BLOCK
    s_rows, t_rows = src_len // LANES, tgt_len // LANES
    log_rows = math.log2(src_len * n_row)
    log_cols = math.log2(tgt_len * n_col)

    def tails(blocks):
        return pltpu.VMEM((blocks, 16, BLOCK), BF16)

    def line(blocks, rows=8):
        return pltpu.VMEM((blocks, rows, BLOCK), F32)

    def side_refs(rows):
        return (
            pltpu.SMEM(slots.shape, jnp.int32),
            pltpu.VMEM((rows, LANES), F32),
            pltpu.SemaphoreType.DMA((2,)),
        )

    def exchange(x, axis, parts, groups=None):
        width = x.shape[0] // parts * LANES
        y = lax.all_to_all(
            x.reshape(parts, width), axis, 0, 0, axis_index_groups=groups, tiled=True
        )
        return y.reshape(-1, LANES)

    def rows_of(n):
        return jax.ShapeDtypeStruct((n, LANES), F32)

    lse, xs = pl.pallas_call(
        functools.partial(src_kernel, other),
        out_shape=(
            rows_of(other * s_rows),
            jax.ShapeDtypeStruct((s_blocks, 3 * DIM, BLOCK), BF16),
        ),
        in_specs=[scalar()] + [far()] * 4,
        out_specs=tuple(whole(2)),
        scratch_shapes=[
            pltpu.SMEM(slots.shape, jnp.int32),
            pltpu.VMEM(src_latent.shape, BF16),
            pltpu.VMEM(tgt_latent.shape, BF16),
            pltpu.VMEM((1, tgt_len), F32),
            pltpu.SemaphoreType.DMA((4,)),
            tails(t_blocks), line(s_blocks + 1), line(s_blocks + 1)],
        compiler_params=pltpu.CompilerParams(vmem_limit_bytes=VMEM_LIMIT),
        name="src_pass",
    )(count, slots, *[
        pltpu.with_memory_space_constraint(a, pltpu.HBM)
        for a in (src_latent, tgt_latent, g_start.reshape(1, -1))
    ])
    lse = exchange(lse, "col", other, groups_z)
    lse = pl.pallas_call(
        functools.partial(merge_kernel, other),
        out_shape=rows_of(side * s_rows),
        in_specs=whole(1),
        out_specs=whole(1)[0],
        compiler_params=pltpu.CompilerParams(vmem_limit_bytes=VMEM_LIMIT),
        name="src_merge",
    )(lse)
    lse = exchange(lse, "col", side, groups_y)
    f_new, lse = pl.pallas_call(
        functools.partial(tgt_kernel, side, n_row, log_rows),
        out_shape=(rows_of(s_rows), rows_of(n_row * t_rows)),
        in_specs=[scalar(), far()] + whole(4),
        out_specs=(far(), whole(1)[0]),
        scratch_shapes=[*side_refs(s_rows), tails(s_blocks), line(t_blocks + 1), line(t_blocks + 1)],
        compiler_params=pltpu.CompilerParams(vmem_limit_bytes=VMEM_LIMIT),
        name="tgt_pass",
    )(count, slots, lse, xs, src_latent, tgt_latent)
    lse = exchange(lse, "row", n_row)
    g_new, means = pl.pallas_call(
        functools.partial(bary_kernel, n_row, log_cols),
        out_shape=(rows_of(t_rows), rows_of(n_col * PACK)),
        in_specs=[scalar(), far()] + whole(3),
        out_specs=(far(), whole(1)[0]),
        scratch_shapes=[
            *side_refs(t_rows),
            tails(t_blocks),
            line(s_blocks + 1, 1),
            pltpu.VMEM((s_blocks + 1, 48, BLOCK), F32),
        ],
        compiler_params=pltpu.CompilerParams(vmem_limit_bytes=VMEM_LIMIT),
        name="bary_pass",
    )(count, slots, lse, xs, tgt_latent)
    means = exchange(means, "col", n_col)
    means = pl.pallas_call(
        functools.partial(mean_kernel, n_col),
        out_shape=rows_of(n_col * 16),
        in_specs=whole(1),
        out_specs=whole(1)[0],
        compiler_params=pltpu.CompilerParams(vmem_limit_bytes=VMEM_LIMIT),
        name="bary_merge",
    )(means)
    means = exchange(means, "col", n_col)
    tiles = pl.pallas_call(
        place_kernel,
        out_shape=jax.ShapeDtypeStruct((DIM // 8, s_rows, 8, LANES), F32),
        in_specs=whole(1),
        out_specs=far(),
        scratch_shapes=[pltpu.SemaphoreType.DMA((8,))],
        compiler_params=pltpu.CompilerParams(vmem_limit_bytes=VMEM_LIMIT),
        name="bary_place",
    )(means.reshape(s_rows, 2, 2, 8, LANES))
    bary = tiles.transpose(0, 2, 1, 3).reshape(DIM, src_len)
    return f_new.reshape(-1), g_new.reshape(-1), bary


def solution(mesh):
    in_specs = (
        P(None, "row"),
        P(None, "col"),
        P("col"),
        P("row", "col", None, None),
        P("row", "col"),
    )
    out_specs = (P("row"), P("col"), P(None, "row"))
    return jax.shard_map(body, mesh=mesh, in_specs=in_specs, out_specs=out_specs, check_vma=False)
```

```python
import functools
import math

import jax
import jax.numpy as jnp
from jax import lax
from jax.experimental import pallas as pl
from jax.experimental.pallas import tpu as pltpu
from jax.sharding import PartitionSpec as P

BLOCK = 512
LANES = 128
DIM = 32
DEPTH = 112
PACK = 17
LATE = 0
HOLD = 5000
VMEM_LIMIT = 16 * 2**20

epsilon = 0.01
very_low = -1e30
log2e = math.log2(math.e)
unit = epsilon / log2e
cross_scale = 2.0 / (DIM * unit)
square_scale = 1.0 / (DIM * unit)

F32 = jnp.float32
BF16 = jnp.bfloat16


def pieces(vec):
    first = vec.astype(BF16).astype(F32)
    rest = vec - first
    second = rest.astype(BF16).astype(F32)
    return first, second, rest - second


def bias_rows(vec):
    row = lax.broadcasted_iota(jnp.int32, (16, vec.shape[1]), 0)
    a, b, c = pieces(vec)
    return jnp.where(row == 0, a, jnp.where(row == 1, b, jnp.where(row == 2, c, 0.0))).astype(BF16)


def one_rows(width):
    row = lax.broadcasted_iota(jnp.int32, (16, width), 0)
    return jnp.where(row < 3, 1.0, 0.0).astype(BF16)


def fill_src(x_ref, xs_ref):
    for b in range(xs_ref.shape[0]):
        xs = x_ref[:, b * BLOCK : (b + 1) * BLOCK].astype(F32) * cross_scale
        for k, piece in enumerate(pieces(xs)):
            xs_ref[b, k * DIM : (k + 1) * DIM, :] = piece.astype(BF16)


def src_operand(xs_ref, s, tail):
    return jnp.concatenate([xs_ref[s], tail], axis=0)


def tgt_block(y_ref, t):
    return y_ref[:, pl.ds(pl.multiple_of(t * BLOCK, BLOCK), BLOCK)]


def tgt_operand(y_ref, t, tail):
    block = tgt_block(y_ref, t)
    return jnp.concatenate([block, block, block, tail], axis=0)


def tile_scores(left, right):
    return lax.dot_general(left, right, (((0,), (0,)), ((), ())), preferred_element_type=F32)


CHUNK = 128


UNROLL = 4
BARY_UNROLL = 2


def tile_lse(left, right):
    top = total = None
    scores = tile_scores(left, right)
    for c in range(0, BLOCK, CHUNK):
        score = scores[c : c + CHUNK, :].reshape(CHUNK // 8, 8, BLOCK)
        most = jnp.max(score, axis=0)
        old, top = top, most if c == 0 else jnp.maximum(top, most)
        part = jnp.sum(jnp.exp2(score - top), axis=0)
        total = part if c == 0 else total * jnp.exp2(old - top) + part
    return top, total


def add_tile(tile, top_ref, total_ref, at):
    top, total = tile
    old = top_ref[at]
    most = jnp.maximum(old, top)
    total_ref[at] = total_ref[at] * jnp.exp2(old - most) + total * jnp.exp2(top - most)
    top_ref[at] = most


def lse_tiles(count, slots, left_of, right_of, at_of, spare, top_ref, total_ref):
    def step(q, carry):
        tiles = []
        for u in range(UNROLL):
            p = q * UNROLL + u
            live = p < count
            p = jnp.minimum(p, count - 1)
            s, t = slots[0, p], slots[1, p]
            tiles.append((tile_lse(left_of(s, t), right_of(s, t)), jnp.where(live, at_of(s, t), spare)))
        for tile, at in tiles:
            add_tile(tile, top_ref, total_ref, at)
        return carry

    lax.fori_loop(0, lax.div(count + UNROLL - 1, UNROLL), step, 0)


def joined(top, total):
    most = jnp.max(top, axis=0, keepdims=True)
    total = jnp.sum(total * jnp.exp2(top - most), axis=0, keepdims=True)
    return jnp.where(total > 0.0, most + jnp.log2(total), very_low)


def clear(top_ref, total_ref):
    top_ref[...] = jnp.full(top_ref.shape, very_low, F32)
    total_ref[...] = jnp.zeros(total_ref.shape, F32)


def spread_rows(blocks, top_ref, total_ref, out_ref, copies):
    per = BLOCK // LANES
    rows = blocks * per
    for b in range(blocks):
        lse = joined(top_ref[b], total_ref[b])
        for k in range(per):
            out_ref[b * per + k : b * per + k + 1, :] = lse[:, k * LANES : (k + 1) * LANES]
    value = out_ref[0:rows, :]
    for c in range(1, copies):
        out_ref[c * rows : (c + 1) * rows, :] = value


def merged(in_ref, parts):
    rows = in_ref.shape[0] // parts
    values = [in_ref[c * rows : (c + 1) * rows, :] for c in range(parts)]
    top = functools.reduce(jnp.maximum, values)
    total = functools.reduce(jnp.add, [jnp.exp2(v - top) for v in values])
    return top + jnp.log2(total)


def fetch(sources, targets, sems):
    copies = [
        pltpu.make_async_copy(source, target, sems.at[k])
        for k, (source, target) in enumerate(zip(sources, targets))
    ]
    for copy in copies:
        copy.start()
    return copies


def src_kernel(parts, count, slots_in, x_in, y_in, g_in, out_ref, xs_ref, slots, x_ref, y_ref, g_ref, sems, bias_ref, top_ref, total_ref):
    copies = fetch(
        (x_in, y_in, g_in, slots_in), (x_ref, y_ref, g_ref, slots), sems
    )
    clear(top_ref, total_ref)
    for copy in copies[1:]:
        copy.wait()
    for b in range(bias_ref.shape[0]):
        ys = y_ref[:, b * BLOCK : (b + 1) * BLOCK].astype(F32)
        square = jnp.sum(ys * ys, axis=0, keepdims=True)
        start = g_ref[:, b * BLOCK : (b + 1) * BLOCK]
        bias_ref[b] = bias_rows(start / unit - square * square_scale)
    copies[0].wait()
    fill_src(x_ref, xs_ref)
    ones = one_rows(BLOCK)
    blocks = xs_ref.shape[0]
    lse_tiles(
        count[0, 0],
        slots,
        lambda s, t: tgt_operand(y_ref, t, bias_ref[t]),
        lambda s, t: src_operand(xs_ref, s, ones),
        lambda s, t: s,
        blocks,
        top_ref,
        total_ref,
    )
    spread_rows(blocks, top_ref, total_ref, out_ref, parts)


def merge_kernel(parts, in_ref, out_ref):
    value = merged(in_ref, parts)
    rows = value.shape[0]
    for c in range(parts):
        out_ref[c * rows : (c + 1) * rows, :] = value


def tgt_kernel(parts, copies, log_rows, count, slots_in, in_ref, xs_ref, x_ref, y_ref, f_out, out_ref, slots, f_ref, sems, bias_ref, top_ref, total_ref):
    fetched = fetch((slots_in,), (slots,), sems)[0]
    clear(top_ref, total_ref)
    bias = -log_rows - merged(in_ref, parts)
    per = BLOCK // LANES
    for b in range(bias_ref.shape[0]):
        xs = x_ref[:, b * BLOCK : (b + 1) * BLOCK].astype(F32)
        square = jnp.sum(xs * xs, axis=0, keepdims=True)
        for k in range(per):
            row = b * per + k
            lanes = slice(k * LANES, (k + 1) * LANES)
            one = bias[row : row + 1, :]
            bias_ref[b, :, lanes] = bias_rows(one)
            f_ref[row : row + 1, :] = unit * one + square[:, lanes] * (1.0 / DIM)
    written = pltpu.make_async_copy(f_ref, f_out, sems.at[1])
    fetched.wait()
    written.start()
    ones = one_rows(BLOCK)
    blocks = y_ref.shape[1] // BLOCK
    lse_tiles(
        count[0, 0],
        slots,
        lambda s, t: src_operand(xs_ref, s, bias_ref[s]),
        lambda s, t: tgt_operand(y_ref, t, ones),
        lambda s, t: t,
        blocks,
        top_ref,
        total_ref,
    )
    spread_rows(blocks, top_ref, total_ref, out_ref, copies)
    written.wait()


def bary_kernel(parts, log_cols, count, slots_in, in_ref, xs_ref, y_ref, g_out, out_ref, slots, g_ref, sems, bias_ref, top_ref, acc_ref):
    fetched = fetch((slots_in,), (slots,), sems)[0]
    top_ref[...] = jnp.full(top_ref.shape, very_low, F32)
    acc_ref[...] = jnp.zeros(acc_ref.shape, F32)
    bias = -log_cols - merged(in_ref, parts)
    per = BLOCK // LANES
    for b in range(bias_ref.shape[0]):
        ys = y_ref[:, b * BLOCK : (b + 1) * BLOCK].astype(F32)
        square = jnp.sum(ys * ys, axis=0, keepdims=True)
        for k in range(per):
            row = b * per + k
            lanes = slice(k * LANES, (k + 1) * LANES)
            one = bias[row : row + 1, :]
            bias_ref[b, :, lanes] = bias_rows(one)
            g_ref[row : row + 1, :] = unit * one + square[:, lanes] * (1.0 / DIM)
    written = pltpu.make_async_copy(g_ref, g_out, sems.at[1])
    fetched.wait()
    written.start()

    @pl.when(lax.rem(lax.axis_index("row"), 2) == LATE)
    def _():
        pl.delay(HOLD)

    spare = xs_ref.shape[0]
    ones = one_rows(BLOCK)
    first_row = lax.broadcasted_iota(jnp.int32, (16, BLOCK), 0) == 0
    total_row = jnp.where(first_row, 1.0, 0.0).astype(BF16)

    def step(q, carry):
        work = []
        for u in range(BARY_UNROLL):
            p = q * BARY_UNROLL + u
            live = p < count[0, 0]
            p = jnp.minimum(p, count[0, 0] - 1)
            s, t = slots[0, p], slots[1, p]
            scores = tile_scores(tgt_operand(y_ref, t, bias_ref[t]), src_operand(xs_ref, s, ones))
            values = jnp.concatenate([tgt_block(y_ref, t), total_row], axis=0)
            work.append([scores, values, None, None, jnp.where(live, s, spare)])
        for item in work:
            for c in range(0, BLOCK, CHUNK):
                scores, values, top, part, at = item
                score = scores[c : c + CHUNK, :]
                most = jnp.max(score, axis=0, keepdims=True)
                old, top = top, most if c == 0 else jnp.maximum(top, most)
                weight = jnp.exp2(score - top).astype(BF16)
                more = jnp.dot(values[:, c : c + CHUNK], weight, preferred_element_type=F32)[0:40, :]
                part = more if c == 0 else part * jnp.exp2(old - top) + more
                item[2:4] = top, part
        tiles = [item[2:] for item in work]
        for top, part, at in tiles:
            old = top_ref[at]
            most = jnp.maximum(old, top)
            acc_ref[at] = acc_ref[at] * jnp.exp2(old - most) + part * jnp.exp2(top - most)
            top_ref[at] = most
        return carry

    lax.fori_loop(0, lax.div(count[0, 0] + BARY_UNROLL - 1, BARY_UNROLL), step, 0)
    for b in range(spare):
        total = acc_ref[b, 32:33, :]
        live = total > 0.0
        lse = jnp.where(live, top_ref[b] + jnp.log2(total), very_low)
        mean = acc_ref[b, 0:32, :] * jnp.where(live, 1.0 / total, 0.0)
        for k in range(per):
            lanes = slice(k * LANES, (k + 1) * LANES)
            for h in range(2):
                at = ((b * per + k) * 2 + h) * PACK
                out_ref[at : at + 16, :] = mean[h * 16 : h * 16 + 16, lanes]
                out_ref[at + 16 : at + 17, :] = lse[:, lanes]
    written.wait()

def mean_kernel(parts, in_ref, out_ref):
    logs = [in_ref[c * PACK + 16 : c * PACK + 17, :] for c in range(parts)]
    top = functools.reduce(jnp.maximum, logs)
    total = jnp.zeros_like(top)
    value = jnp.zeros((16, LANES), F32)
    for c in range(parts):
        weight = jnp.exp2(logs[c] - top)
        total = total + weight
        value = value + weight * in_ref[c * PACK : c * PACK + 16, :]
    value = value / total
    for c in range(parts):
        out_ref[c * 16 : (c + 1) * 16, :] = value


def place_kernel(in_ref, out_ref, sems):
    half = in_ref.shape[0] // 2
    copies = []
    for d in range(4):
        for k in range(2):
            runs = pl.ds(k * half, half)
            copies.append(
                pltpu.make_async_copy(
                    in_ref.at[runs, d // 2, d % 2], out_ref.at[d, runs], sems.at[2 * d + k]
                )
            )
    for copy in copies:
        copy.start()
    for copy in copies:
        copy.wait()


def whole(count):
    return [pl.BlockSpec(memory_space=pltpu.VMEM)] * count


def scalar():
    return pl.BlockSpec(memory_space=pltpu.SMEM)


def far():
    return pl.BlockSpec(memory_space=pltpu.HBM)


def body(src_latent, tgt_latent, g_start, pairs, counts):
    src_len = src_latent.shape[1]
    tgt_len = tgt_latent.shape[1]
    n_row, n_col = lax.axis_size("row"), lax.axis_size("col")
    side = 8
    other = n_col // side
    groups_z = [[z * side + y for z in range(other)] for y in range(side)]
    groups_y = [[z * side + y for y in range(side)] for z in range(other)]
    slots = pltpu.with_memory_space_constraint(pairs.reshape(pairs.shape[2:]).T, pltpu.HBM)
    count = counts
    s_blocks, t_blocks = src_len // BLOCK, tgt_len // BLOCK
    s_rows, t_rows = src_len // LANES, tgt_len // LANES
    log_rows = math.log2(src_len * n_row)
    log_cols = math.log2(tgt_len * n_col)

    def tails(blocks):
        return pltpu.VMEM((blocks, 16, BLOCK), BF16)

    def line(blocks, rows=8):
        return pltpu.VMEM((blocks, rows, BLOCK), F32)

    def side_refs(rows):
        return (
            pltpu.SMEM(slots.shape, jnp.int32),
            pltpu.VMEM((rows, LANES), F32),
            pltpu.SemaphoreType.DMA((2,)),
        )

    def exchange(x, axis, parts, groups=None):
        width = x.shape[0] // parts * LANES
        y = lax.all_to_all(
            x.reshape(parts, width), axis, 0, 0, axis_index_groups=groups, tiled=True
        )
        return y.reshape(-1, LANES)

    def rows_of(n):
        return jax.ShapeDtypeStruct((n, LANES), F32)

    lse, xs = pl.pallas_call(
        functools.partial(src_kernel, other),
        out_shape=(
            rows_of(other * s_rows),
            jax.ShapeDtypeStruct((s_blocks, 3 * DIM, BLOCK), BF16),
        ),
        in_specs=[scalar()] + [far()] * 4,
        out_specs=tuple(whole(2)),
        scratch_shapes=[
            pltpu.SMEM(slots.shape, jnp.int32),
            pltpu.VMEM(src_latent.shape, BF16),
            pltpu.VMEM(tgt_latent.shape, BF16),
            pltpu.VMEM((1, tgt_len), F32),
            pltpu.SemaphoreType.DMA((4,)),
            tails(t_blocks), line(s_blocks + 1), line(s_blocks + 1)],
        compiler_params=pltpu.CompilerParams(vmem_limit_bytes=VMEM_LIMIT),
        name="src_pass",
    )(count, slots, *[
        pltpu.with_memory_space_constraint(a, pltpu.HBM)
        for a in (src_latent, tgt_latent, g_start.reshape(1, -1))
    ])
    lse = exchange(lse, "col", other, groups_z)
    lse = pl.pallas_call(
        functools.partial(merge_kernel, other),
        out_shape=rows_of(side * s_rows),
        in_specs=whole(1),
        out_specs=whole(1)[0],
        compiler_params=pltpu.CompilerParams(vmem_limit_bytes=VMEM_LIMIT),
        name="src_merge",
    )(lse)
    lse = exchange(lse, "col", side, groups_y)
    f_new, lse = pl.pallas_call(
        functools.partial(tgt_kernel, side, n_row, log_rows),
        out_shape=(rows_of(s_rows), rows_of(n_row * t_rows)),
        in_specs=[scalar(), far()] + whole(4),
        out_specs=(far(), whole(1)[0]),
        scratch_shapes=[*side_refs(s_rows), tails(s_blocks), line(t_blocks + 1), line(t_blocks + 1)],
        compiler_params=pltpu.CompilerParams(vmem_limit_bytes=VMEM_LIMIT),
        name="tgt_pass",
    )(count, slots, lse, xs, src_latent, tgt_latent)
    lse = exchange(lse, "row", n_row)
    g_new, means = pl.pallas_call(
        functools.partial(bary_kernel, n_row, log_cols),
        out_shape=(rows_of(t_rows), rows_of(n_col * PACK)),
        in_specs=[scalar(), far()] + whole(3),
        out_specs=(far(), whole(1)[0]),
        scratch_shapes=[
            *side_refs(t_rows),
            tails(t_blocks),
            line(s_blocks + 1, 1),
            pltpu.VMEM((s_blocks + 1, 40, BLOCK), F32),
        ],
        compiler_params=pltpu.CompilerParams(vmem_limit_bytes=VMEM_LIMIT),
        name="bary_pass",
    )(count, slots, lse, xs, tgt_latent)
    means = exchange(means, "col", n_col)
    means = pl.pallas_call(
        functools.partial(mean_kernel, n_col),
        out_shape=rows_of(n_col * 16),
        in_specs=whole(1),
        out_specs=whole(1)[0],
        compiler_params=pltpu.CompilerParams(vmem_limit_bytes=VMEM_LIMIT),
        name="bary_merge",
    )(means)
    means = exchange(means, "col", n_col)
    tiles = pl.pallas_call(
        place_kernel,
        out_shape=jax.ShapeDtypeStruct((DIM // 8, s_rows, 8, LANES), F32),
        in_specs=whole(1),
        out_specs=far(),
        scratch_shapes=[pltpu.SemaphoreType.DMA((8,))],
        compiler_params=pltpu.CompilerParams(vmem_limit_bytes=VMEM_LIMIT),
        name="bary_place",
    )(means.reshape(s_rows, 2, 2, 8, LANES))
    bary = tiles.transpose(0, 2, 1, 3).reshape(DIM, src_len)
    return f_new.reshape(-1), g_new.reshape(-1), bary


def solution(mesh):
    in_specs = (
        P(None, "row"),
        P(None, "col"),
        P("col"),
        P("row", "col", None, None),
        P("row", "col"),
    )
    out_specs = (P("row"), P("col"), P(None, "row"))
    return jax.shard_map(body, mesh=mesh, in_specs=in_specs, out_specs=out_specs, check_vma=False)
```
